256 devices in a mesh: stream: 2 (over z_hi), dp: 16 (over x, y), tensor: 8 (over z_lo, core).
Axes of the slice: x: 4, y: 4, z: 8 (z_hi: 2, z_lo: 4; z = z_hi * 4 + z_lo), core: 2. Of those that a mesh axis runs over, the one named last changes fastest.
Arguments:
- hidden: bfloat16 [2, 256, 8192], P('stream', 'tensor', 'dp'), may hold values from -3 to 3
- cached_rotated_keys: bfloat16 [2, 256, 8, 256, 128], P('stream', 'dp', 'tensor'), may hold values from -6 to 6
- cached_values: bfloat16 [2, 256, 8, 256, 128], P('stream', 'dp', 'tensor'), may hold values from -18 to 18
- cache_lengths: int32 [2, 256], P('stream', 'dp'), may hold values from 1 to 256, as said below
- recent_ids: int32 [256, 128], replicated, may hold values from 0 to 65535
- guidance: float32 [256], replicated, may hold values from 1 to 3
- w_query: bfloat16 [8192, 8192], P('dp', 'tensor'), may hold values from -0.0625 to 0.0625
- key_value_weight: bfloat16 [8192, 2, 1024], P('dp', None, 'tensor'), may hold values from -0.0625 to 0.0625
- w_output: bfloat16 [8192, 8192], P('tensor', 'dp'), may hold values from -0.0625 to 0.0625
- norm_gain: bfloat16 [8192], P('dp'), may hold values from 0.5 to 1.5
- w_head: bfloat16 [8192, 65536], P(None, ('dp', 'tensor')), may hold values from -0.16503906 to 0.16503906
Outputs:
- guided_logprobs: float32 [256, 65536], P('stream', ('dp', 'tensor'))
The draws below stay inside these ranges and needn't reach their ends.
Inputs may be any that keep to these rules, and one draw needn't show every extreme that they name: `cache_lengths`: every prompt has 1 to 256 filled slots in each stream; some prompt has all 256; lengths differ widely from one group of 16 prompts to the next.
All inputs are finite; a program needn't handle non-finite values.
Results may differ from the reference program's by a relative error of at most 0.0025.
Values may be sent and summed in bfloat16 or wider, within the bound.
A program may use at most 64 MiB of HBM per device.

```python
import math
import jax
import jax.numpy as jnp
import numpy as np
from jax import lax

MODEL_WIDTH = 8192
QUERY_HEADS = 64
KEY_VALUE_HEADS = 8
HEAD_SIZE = 128
PROMPT_DEV = 16
CACHE_SLOTS = 256
RECENT = 128
PROMPT_COUNT = 256
VOCAB = 65536


def draw_cache_lengths(key, part):
    first_key, second_key = jax.random.split(jax.random.fold_in(key, 71))
    blocks = PROMPT_COUNT // PROMPT_DEV
    ceiling = jax.random.randint(first_key, (2, blocks, 1), CACHE_SLOTS // 4, CACHE_SLOTS + 1)
    ceiling = jnp.broadcast_to(ceiling, (2, blocks, PROMPT_DEV)).reshape(2, PROMPT_COUNT)
    raw_draw = jax.random.randint(second_key, (2, PROMPT_COUNT), 0, 1048576)
    lengths = 1 + raw_draw % ceiling
    lengths = lengths.at[:, 0].set(CACHE_SLOTS)
    return lengths.astype(jnp.int32)


def touch_ends(result, rng, low, top_value):
    extent = result.shape
    index_at = [jax.random.randint(jax.random.fold_in(rng, axis), (), 0, extent[axis]) for axis in range(len(extent))]
    result = result.at[tuple(index_at)].set(low)
    longest = extent.index(max(extent))
    index_at[longest] = (index_at[longest] + 1) % extent[longest]
    return result.at[tuple(index_at)].set(top_value)


def block_scale(own_key, extent, cuts, low, high):
    level, own = 1.0, jax.random.fold_in(own_key, 6)
    for axis_at, blocks in cuts:
        steps = jnp.exp(jax.random.uniform(jax.random.fold_in(own, axis_at), (blocks,), jnp.float32, low / len(cuts), high / len(cuts)))
        level = level * jnp.repeat(steps, extent[axis_at] // blocks).reshape([-1 if axis == axis_at else 1 for axis in range(len(extent))])
    return level


def rank_bounds(number_of, skew):
    weights = [(1 << 20) // math.isqrt(standing ** skew) + 1 for standing in range(1, number_of + 1)]
    scale = 1 + sum(weights) // (1 << 30)
    return np.cumsum(np.array([max(1, weight // scale) for weight in weights]))


def ranked(stream_key, extent, count, skew):
    table = rank_bounds(count, skew)
    ticket = jax.random.randint(jax.random.fold_in(stream_key, 1), extent, 0, int(table[count - 1]))
    standing = jnp.searchsorted(jnp.asarray(table, jnp.int32), ticket, side="right")
    return jax.random.permutation(jax.random.fold_in(stream_key, 2), count)[standing].astype(jnp.int32)


def scatter_about(stream_key, shape, width, most, pieces=(), kind=jnp.bfloat16):
    gain = block_scale(stream_key, shape, pieces, -0.22, 0.18) if pieces else 1.0
    result = jax.random.normal(stream_key, shape, jnp.float32) * width * gain
    return jnp.minimum(jnp.maximum(result, -most), most).astype(kind)


def setup_inputs(seed: int = 0) -> dict:
    key_of = jax.random.split(jax.random.key(seed), 12)
    return {
        "hidden": scatter_about(key_of[0], (2, PROMPT_COUNT, MODEL_WIDTH), 0.5, 3.0, ((0, 2), (1, 8), (2, 16))),
        "cached_rotated_keys": scatter_about(key_of[1], (2, PROMPT_COUNT, KEY_VALUE_HEADS, CACHE_SLOTS, HEAD_SIZE), 1.0, 6.0, ((0, 2), (1, 16), (2, 8))),
        "cached_values": scatter_about(key_of[2], (2, PROMPT_COUNT, KEY_VALUE_HEADS, CACHE_SLOTS, HEAD_SIZE), 3.0, 18.0, ((0, 2), (1, 16), (2, 8))),
        "cache_lengths": draw_cache_lengths(jax.random.fold_in(key_of[11], 71), 0),
        "recent_ids": touch_ends(ranked(key_of[4], (PROMPT_COUNT, RECENT), VOCAB, 4), jax.random.fold_in(key_of[4], 3), 0, VOCAB - 1).astype(jnp.int32),
        "guidance": jnp.clip(jnp.exp(jax.random.uniform(key_of[5], (PROMPT_COUNT,), jnp.float32, math.log(1.0), math.log(3.0))), 1.0, 3.0),
        "w_query": scatter_about(key_of[6], (MODEL_WIDTH, QUERY_HEADS * HEAD_SIZE), MODEL_WIDTH ** -0.5, 0.0625, ((0, 16), (1, 8))),
        "key_value_weight": scatter_about(key_of[7], (MODEL_WIDTH, 2, KEY_VALUE_HEADS * HEAD_SIZE), MODEL_WIDTH ** -0.5, 0.0625, ((0, 16), (2, 8))),
        "w_output": scatter_about(key_of[8], (QUERY_HEADS * HEAD_SIZE, MODEL_WIDTH), (QUERY_HEADS * HEAD_SIZE) ** -0.5, 0.0625, ((0, 8), (1, 16))),
        "norm_gain": jnp.clip(1.0 + 0.1 * jax.random.normal(key_of[9], (MODEL_WIDTH,), jnp.float32), 0.5, 1.5).astype(jnp.bfloat16),
        "w_head": scatter_about(key_of[10], (MODEL_WIDTH, VOCAB), (2.5 * MODEL_WIDTH ** -0.5), 0.16503906, ((1, 128),)),
    }


rope_theta = 500000.0
penalty_step = 1.5
norm_eps = 1e-05

def rotate(values, positions):
    halfway = values.shape[-1] // 2
    frequency = rope_theta ** (-(jnp.arange(halfway, dtype=jnp.float32) * 2.0 / values.shape[-1]))
    angles = positions.astype(jnp.float32)[:, None, None] * frequency
    cosine_term = jnp.cos(angles)
    sine_term = jnp.sin(angles)
    first_half = values[..., :halfway]
    second_half = values[..., halfway:]
    return jnp.concatenate([first_half * cosine_term - second_half * sine_term, second_half * cosine_term + first_half * sine_term], axis=-1)

def stream_logits(operands, w_query, key_value_weight, w_output, norm_gain, w_head):
    hidden_state_rows, key_cache, value_cache, lengths = operands
    batch_rows = hidden_state_rows.shape[0]
    queries = jnp.dot(hidden_state_rows, w_query, preferred_element_type=jnp.float32)
    key_value_rows = jnp.dot(hidden_state_rows, key_value_weight.reshape(MODEL_WIDTH, 2 * KEY_VALUE_HEADS * HEAD_SIZE), preferred_element_type=jnp.float32).reshape(batch_rows, 2, KEY_VALUE_HEADS, HEAD_SIZE)
    rotated_query = rotate(queries.reshape(batch_rows, QUERY_HEADS, HEAD_SIZE), lengths).astype(jnp.bfloat16)
    fresh_key = rotate(key_value_rows[:, 0], lengths).astype(jnp.bfloat16)
    value_new = key_value_rows[:, 1].astype(jnp.bfloat16)
    grouped_queries = rotated_query.reshape(batch_rows, KEY_VALUE_HEADS, QUERY_HEADS // KEY_VALUE_HEADS, HEAD_SIZE).astype(jnp.float32)
    attention_scale = HEAD_SIZE ** (-0.5)
    scores = jnp.einsum('bkgd,bksd->bkgs', grouped_queries, key_cache.astype(jnp.float32)) * attention_scale
    self_score = jnp.einsum('wxuz,wxz->wxu', grouped_queries, fresh_key.astype(jnp.float32)) * attention_scale
    valid = jnp.arange(CACHE_SLOTS, dtype=jnp.int32)[None, :] < lengths[:, None]
    exps = jnp.where(valid[:, None, None, :], jnp.exp(scores), 0.0)
    own_exp = jnp.exp(self_score)
    denominator = lax.optimization_barrier(jnp.sum(exps, -1)) + own_exp
    weights = (exps / denominator[..., None]).astype(jnp.bfloat16)
    own_weight = (own_exp / denominator).astype(jnp.bfloat16)
    attended = jnp.einsum('bkgs,bksd->bkgd', weights.astype(jnp.float32), value_cache.astype(jnp.float32))
    attended = attended + own_weight.astype(jnp.float32)[..., None] * value_new.astype(jnp.float32)[:, :, None, :]
    attended = attended.reshape(batch_rows, QUERY_HEADS * HEAD_SIZE).astype(jnp.bfloat16)
    projected = jnp.dot(attended, w_output, preferred_element_type=jnp.float32)
    residual = (hidden_state_rows.astype(jnp.float32) + projected).astype(jnp.bfloat16)
    widened = residual.astype(jnp.float32)
    squares = lax.optimization_barrier(jnp.sum(widened * widened, 1))
    inverse = lax.rsqrt(squares / MODEL_WIDTH + norm_eps)
    normed = (widened * inverse[:, None] * norm_gain.astype(jnp.float32)).astype(jnp.bfloat16)
    return jnp.dot(normed, w_head, preferred_element_type=jnp.float32)

def reference(hidden, cached_rotated_keys, cached_values, cache_lengths, recent_ids, guidance, w_query, key_value_weight, w_output, norm_gain, w_head):

    def per_stream(operands):
        return stream_logits(operands, w_query, key_value_weight, w_output, norm_gain, w_head)
    logits = lax.map(per_stream, (hidden, cached_rotated_keys, cached_values, cache_lengths))
    conditional = logits[0]
    unconditional = logits[1]
    guided = unconditional + guidance[:, None] * (conditional - unconditional)

    def add_counts(counts, column_ids):
        hits = (column_ids[:, None] == jnp.arange(VOCAB, dtype=jnp.int32)[None, :]).astype(jnp.float32)
        return (counts + hits, None)
    counts, unused = lax.scan(add_counts, jnp.zeros((PROMPT_COUNT, VOCAB), jnp.float32), recent_ids.T)
    guided = guided - penalty_step * counts
    totals = lax.optimization_barrier(jnp.sum(jnp.exp(guided), 1))
    return guided - jnp.log(totals)[:, None]
```

```python
import jax
import jax.numpy as jnp
from jax import lax
from jax.experimental import pallas as pl
from jax.experimental.pallas import tpu as pltpu
from jax.sharding import PartitionSpec as P

MESH = pl.DeviceIdType.MESH
F32 = jnp.float32
BF16 = jnp.bfloat16
WIDTH = 8192
HEAD = 128
RING = 4
DP = 16
TEN = 8

rope_theta = 500000.0
penalty_step = 1.5
norm_eps = 1e-05


def routes():
    found = []
    for depth in range(5):
        for dx in range(RING):
            for dy in range(RING):
                if min(dx, RING - dx) + min(dy, RING - dy) != depth:
                    continue
                for quarter in range(4):
                    first, second = (dx, dy) if quarter < 2 else (dy, dx)
                    names = ("x", "y") if quarter < 2 else ("y", "x")
                    odd = quarter % 2
                    hops = []
                    if second == 0:
                        if first == 0:
                            hops += [(names[0], 1), (names[0], -1)]
                        elif first == 1 and not odd:
                            hops += [(names[0], 1)]
                        elif first == 3 and odd:
                            hops += [(names[0], -1)]
                        hops += [(names[1], 1), (names[1], -1)]
                    elif second == 1 and not odd:
                        hops += [(names[1], 1)]
                    elif second == 3 and odd:
                        hops += [(names[1], -1)]
                    found.append((depth, dx, dy, quarter, hops))
    return found


ROUTES = routes()
N_FORWARD = sum(len(r[4]) for r in ROUTES)
OFFSETS = [
    sorted({(r[1], r[2]) for r in ROUTES if r[0] == depth}) for depth in range(5)
]


def kernel(
    hidden,
    keys,
    vals,
    lens,
    ids,
    guid,
    wq,
    kvw,
    wo,
    gain,
    wh,
    out,
    h_all,
    wq_v,
    kvw_v,
    k_v,
    v_v,
    wo_v,
    wh_v,
    ids_v,
    gain_all,
    part,
    recv_b,
    q_s,
    att_s,
    att_all,
    part_d,
    recv_d,
    resid,
    buf,
    acc,
    ssq,
    counts,
    gcol,
    tot_one,
    tot_t,
    tot_d,
    load_sem,
    a_send,
    a_recv,
    gain_send,
    gain_recv,
    b_send,
    b_recv,
    c_send,
    c_recv,
    d_send,
    d_recv,
    z_send,
    z_recv,
    f_send,
    f_recv,
    sib_send,
    sib_recv,
    t_send,
    t_recv,
    s_send,
    s_recv,
):
    S = lax.axis_index("stream")
    D = lax.axis_index("dp")
    T = lax.axis_index("tensor")
    zl, c = T // 2, T % 2
    x, y = D // RING, D % RING
    sib = (S, D, zl * 2 + 1 - c)

    def remote(src, dst, ssem, rsem, dev):
        copy = pltpu.make_async_remote_copy(
            src_ref=src,
            dst_ref=dst,
            send_sem=ssem,
            recv_sem=rsem,
            device_id=dev,
            device_id_type=MESH,
        )
        copy.start()
        return copy

    def arrived(ref, rsem, ssem):
        pltpu.make_async_remote_copy(
            src_ref=ref,
            dst_ref=ref,
            send_sem=ssem,
            recv_sem=rsem,
            device_id=sib,
            device_id_type=MESH,
        ).wait_recv()

    sent = []

    barrier = pltpu.get_barrier_semaphore()
    for i in range(1, DP):
        pl.semaphore_signal(
            barrier, inc=1, device_id=(S, (D + i) % DP, T), device_id_type=MESH
        )
    for i in range(1, 16):
        other = (S * TEN + T + i) % 16
        pl.semaphore_signal(
            barrier, inc=1, device_id=(other // TEN, D, other % TEN), device_id_type=MESH
        )

    loads = []

    def load(src, dst):
        copy = pltpu.make_async_copy(src, dst, load_sem.at[len(loads)])
        copy.start()
        loads.append(copy)
        return copy

    l_h = load(hidden.at[0], h_all.at[T])
    l_wq = load(wq, wq_v)
    l_kv = load(kvw, kvw_v)
    l_ids = load(ids.at[pl.ds(S * 128, 128), :], ids_v)
    l_k = load(keys.at[0, :, 0], k_v)
    l_v = load(vals.at[0, :, 0], v_v)
    l_wo = load(wo, wo_v)
    pl.semaphore_wait(barrier, 30)

    for dz in (3, 2, 1):
        dev = (S, D, ((zl + dz) % 4) * 2 + c)
        sent.append(remote(hidden.at[0], h_all.at[T], a_send.at[dz], a_recv.at[T], dev))
    sent.append(remote(hidden.at[0], h_all.at[T], a_send.at[0], a_recv.at[T], sib))
    gain_row = gain[...].astype(F32)
    gain_all[D] = gain_row
    l_wh = load(wh, wh_v)
    for n, dz in enumerate((1, 3, 2)):
        src = ((zl + dz) % 4) * 2 + c
        arrived(h_all.at[src], a_recv.at[src], a_send.at[0])
        sent.append(remote(h_all.at[src], h_all.at[src], a_send.at[4 + n], a_recv.at[src], sib))
    l_h.wait()
    l_wq.wait()
    l_kv.wait()
    for dz in range(4):
        src = ((zl + dz) % 4) * 2 + 1 - c
        arrived(h_all.at[src], a_recv.at[src], a_send.at[0])

    h = h_all[...].reshape(256, 512)
    for n in range(4):
        cols = pl.ds(n * 256, 256)
        r = jnp.dot(h, wq_v[:, cols], preferred_element_type=F32)
        part[:, :, cols] = r.reshape(DP, 16, 256).astype(BF16)
    for n in range(2):
        cols = pl.ds(1024 + n * 128, 128)
        r = jnp.dot(h, kvw_v[:, n, :], preferred_element_type=F32)
        part[:, :, cols] = r.reshape(DP, 16, 128).astype(BF16)
    for i in range(1, DP):
        to = (D + i) % DP
        sent.append(remote(part.at[to], recv_b.at[D], b_send.at[i], b_recv.at[D], (S, to, T)))
    for i in range(1, DP):
        to = (D + i) % DP
        sent.append(
            remote(gain_all.at[D], gain_all.at[D], gain_send.at[i], gain_recv.at[D], (S, to, T))
        )

    lane = lax.broadcasted_iota(jnp.int32, (16, HEAD), 1)
    row = lax.broadcasted_iota(jnp.int32, (16, HEAD), 0)
    freq = jnp.exp(((lane % 64).astype(F32) * (2.0 / HEAD)) * (-jnp.log(F32(rope_theta))))
    position = jnp.zeros((16, HEAD), jnp.int32)
    for p in range(16):
        position = jnp.where(row == p, lens[0, p], position)
    angle = position.astype(F32) * freq
    cosine = jnp.cos(angle)
    sine = jnp.sin(angle) * jnp.where(lane < 64, -1.0, 1.0)

    l_ids.wait()
    base = (D * TEN + T) * 512
    ids_v[...] = jnp.transpose(ids_v[...]) - base
    for n in range(4):
        column = lax.broadcasted_iota(jnp.int32, (128, 128), 0) + n * 128

        def add(r, total):
            for k in range(8):
                here = ids_v[pl.ds(r * 8 + k, 1), :]
                total = total + jnp.where(column == here, 1.0, 0.0)
            return total

        total = lax.fori_loop(0, 16, add, jnp.zeros((128, 128), F32))
        counts[:, pl.ds(n * 128, 128)] = jnp.transpose(total) * penalty_step
    gcol[...] = jnp.transpose(jnp.broadcast_to(guid[pl.ds(S, 1), :], (128, 128)))

    qkv = part[D].astype(F32)
    for i in range(1, DP):
        src = (D + DP - i) % DP
        arrived(recv_b.at[src], b_recv.at[src], b_send.at[i])
        qkv = qkv + recv_b[src].astype(F32)

    def turn(v):
        return v * cosine + pltpu.roll(v, 64, 1) * sine

    for g in range(8):
        q_s[:, g, :] = turn(qkv[:, g * HEAD : (g + 1) * HEAD])
    k_new = turn(qkv[:, 1024:1152]).astype(BF16).astype(F32)
    v_new = qkv[:, 1152:1280].astype(BF16).astype(F32)

    l_k.wait()
    l_v.wait()
    scale = HEAD ** (-0.5)
    slot_at = lax.broadcasted_iota(jnp.int32, (8, 256), 1)
    for p in range(16):
        q = q_s[p].astype(BF16)
        scores = (
            lax.dot_general(q, k_v[p], (((1,), (1,)), ((), ())), preferred_element_type=F32)
            * scale
        )
        own = jnp.sum(q.astype(F32) * k_new[p : p + 1, :], axis=1, keepdims=True) * scale
        e = jnp.where(slot_at < lens[0, p], jnp.exp(scores), 0.0)
        e_own = jnp.exp(own)
        den = jnp.sum(e, axis=1, keepdims=True) + e_own
        w = (e / den).astype(BF16)
        w_own = (e_own / den).astype(BF16).astype(F32)
        o = jnp.dot(w, v_v[p], preferred_element_type=F32) + w_own * v_new[p : p + 1, :]
        att_s[p] = o
    for g in range(8):
        att_all[D, :, pl.ds(g * HEAD, HEAD)] = att_s[:, g, :].astype(BF16)

    def neighbour(name, step):
        if name == "x":
            return (S, ((x + RING + step) % RING) * RING + y, T)
        return (S, x * RING + (y + RING + step) % RING, T)

    def gather(depth, view, send, recv, count, each=None):
        for level, dx, dy, quarter, hops in ROUTES:
            if level != depth:
                continue
            slot = ((x + RING - dx) % RING) * RING + (y + RING - dy) % RING
            piece = view(slot, quarter)
            if depth > 0:
                arrived(piece, recv.at[slot, quarter], send.at[0])
            for hop in hops:
                sent.append(
                    remote(piece, piece, send.at[count], recv.at[slot, quarter], neighbour(*hop))
                )
                count += 1
            if each is not None:
                each(slot, quarter)
        return count

    done = 0
    for depth in range(5):
        done = gather(
            depth,
            lambda slot, quarter: att_all.at[slot, :, pl.ds(quarter * 256, 256)],
            c_send,
            c_recv,
            done,
        )

    l_wo.wait()
    a = att_all[...].reshape(256, 1024)
    for n in range(2):
        cols = pl.ds(n * 256, 256)
        r = jnp.dot(a, wo_v[:, cols], preferred_element_type=F32)
        part_d[:, :, cols] = r.reshape(TEN, 32, 256).astype(BF16)

    def owned(t):
        inner = ((t + 2) // 4) % 2
        half = inner * S + (1 - inner) * (1 - S)
        return half, inner * (t - 2) + (1 - inner) * (t - 4 * (t // 6))

    for i in range(1, TEN):
        to = (T + i) % TEN
        half, j = owned(to)
        sent.append(
            remote(part_d.at[half * 4 + j], recv_d.at[T], d_send.at[i], d_recv.at[T], (S, D, to))
        )
    my_half, my_j = owned(T)
    mine = my_half * 4 + my_j
    total = h_all[mine].astype(F32) + part_d[mine].astype(F32)
    for i in range(1, TEN):
        src = (T + TEN - i) % TEN
        arrived(recv_d.at[src], d_recv.at[src], d_send.at[i])
        total = total + recv_d[src].astype(F32)
    resid[...] = total.astype(BF16)

    place = buf.at[S, D, pl.ds(my_j * 32, 32), :]
    for z in range(4):
        at_home = jnp.logical_and(my_half == S, 2 * z + S == T)

        @pl.when(at_home)
        def _():
            pltpu.make_async_copy(resid, place, z_recv.at[my_j]).start()

        @pl.when(jnp.logical_not(at_home))
        def _():
            remote(resid, place, z_send.at[z], z_recv.at[my_j], (my_half, D, 2 * z + S))

    for i in range(1, DP):
        src = (D + DP - i) % DP
        arrived(gain_all.at[src], gain_recv.at[src], gain_send.at[i])
    l_wh.wait()
    acc[...] = jnp.zeros_like(acc)
    ssq[...] = jnp.zeros_like(ssq)

    def rows(slot, quarter):
        return buf.at[c, slot, pl.ds(quarter * 32, 32), :]

    passed = [0]

    def share(slot, quarter):
        piece = rows(slot, quarter)
        sent.append(
            remote(piece, piece, sib_send.at[passed[0]], sib_recv.at[slot, quarter], sib)
        )
        passed[0] += 1

    def head(depth):
        offsets = OFFSETS[depth]

        def step(i, carry):
            dx, dy = jnp.int32(offsets[0][0]), jnp.int32(offsets[0][1])
            for n, (ox, oy) in enumerate(offsets[1:]):
                dx = jnp.where(i == n + 1, ox, dx)
                dy = jnp.where(i == n + 1, oy, dy)
            slot = ((x + RING - dx) % RING) * RING + (y + RING - dy) % RING
            for quarter in range(4):
                there = buf.at[1 - c, slot, pl.ds(quarter * 32, 32), :]
                arrived(there, sib_recv.at[slot, quarter], sib_send.at[0])
            v = buf[:, slot].reshape(256, 512).astype(F32)
            v2 = v * v
            ssq[...] += (
                v2[:, 0:128] + v2[:, 128:256] + v2[:, 256:384] + v2[:, 384:512]
            )
            w = (v * gain_all[slot]).astype(BF16)
            acc[...] += jnp.dot(
                w, wh_v[pl.ds(pl.multiple_of(slot * 512, 512), 512), :], preferred_element_type=F32
            )
            return carry

        lax.fori_loop(0, len(offsets), step, 0)

    for quarter in range(4):
        arrived(rows(D, quarter), z_recv.at[quarter], z_send.at[0])
    done = 0
    for depth in range(5):
        done = gather(depth, rows, f_send, f_recv, done, share)
        if depth > 0:
            head(depth - 1)
    head(4)

    inv = lax.rsqrt(jnp.sum(ssq[...], axis=1, keepdims=True) / WIDTH + norm_eps)
    cond = acc[0:128, :] * inv[0:128]
    uncond = acc[128:256, :] * inv[128:256]
    guide = gcol[:, 0:1]
    guided = uncond + guide * (cond - uncond) - counts[...]
    acc[0:128, :] = guided
    e = jnp.exp(guided)
    e = e[:, 0:128] + e[:, 128:256] + e[:, 256:384] + e[:, 384:512]
    tot_one[...] = jnp.sum(jnp.transpose(e), axis=0, keepdims=True)
    tot_t[T] = tot_one[...]
    for i in range(1, TEN):
        to = (T + i) % TEN
        sent.append(remote(tot_one, tot_t.at[T], t_send.at[i], t_recv.at[T], (S, D, to)))
    for i in range(1, TEN):
        src = (T + TEN - i) % TEN
        arrived(tot_t.at[src], t_recv.at[src], t_send.at[i])
    tot_d[D] = jnp.sum(tot_t[...], axis=0)
    for i in range(1, DP):
        to = (D + i) % DP
        sent.append(remote(tot_d.at[D], tot_d.at[D], s_send.at[i], s_recv.at[D], (S, to, T)))
    for i in range(1, DP):
        src = (D + DP - i) % DP
        arrived(tot_d.at[src], s_recv.at[src], s_send.at[i])
    log_total = jnp.transpose(jnp.broadcast_to(jnp.log(jnp.sum(tot_d[...], axis=0)), (128, 128)))
    for n in range(4):
        cols = pl.ds(n * 128, 128)
        out[:, cols] = acc[0:128, cols] - log_total

    for copy in sent:
        copy.wait_send()
    for z in range(4):
        at_home = jnp.logical_and(my_half == S, 2 * z + S == T)

        @pl.when(jnp.logical_not(at_home))
        def _():
            pltpu.make_async_remote_copy(
                src_ref=resid,
                dst_ref=place,
                send_sem=z_send.at[z],
                recv_sem=z_recv.at[my_j],
                device_id=(my_half, D, 2 * z + S),
                device_id_type=MESH,
            ).wait_send()


def body(hidden, keys, vals, lens, ids, guid, wq, kvw, wo, gain, wh):
    dma = pltpu.SemaphoreType.DMA
    anywhere = pl.BlockSpec(memory_space=pl.ANY)
    vmem = pl.BlockSpec(memory_space=pltpu.VMEM)
    smem = pl.BlockSpec(memory_space=pltpu.SMEM)
    return pl.pallas_call(
        kernel,
        out_shape=jax.ShapeDtypeStruct((128, 512), F32),
        in_specs=[
            anywhere,
            anywhere,
            anywhere,
            smem,
            anywhere,
            vmem,
            anywhere,
            anywhere,
            anywhere,
            vmem,
            anywhere,
        ],
        out_specs=vmem,
        scratch_shapes=[
            pltpu.VMEM((8, 32, 512), BF16),
            pltpu.VMEM((512, 1024), BF16),
            pltpu.VMEM((512, 2, 128), BF16),
            pltpu.VMEM((16, 256, 128), BF16),
            pltpu.VMEM((16, 256, 128), BF16),
            pltpu.VMEM((1024, 512), BF16),
            pltpu.VMEM((8192, 512), BF16),
            pltpu.VMEM((128, 128), jnp.int32),
            pltpu.VMEM((DP, 1, 512), F32),
            pltpu.VMEM((DP, 16, 1280), BF16),
            pltpu.VMEM((DP, 16, 1280), BF16),
            pltpu.VMEM((16, 8, 128), F32),
            pltpu.VMEM((16, 8, 128), F32),
            pltpu.VMEM((DP, 16, 1024), BF16),
            pltpu.VMEM((TEN, 32, 512), BF16),
            pltpu.VMEM((TEN, 32, 512), BF16),
            pltpu.VMEM((32, 512), BF16),
            pltpu.VMEM((2, DP, 128, 512), BF16),
            pltpu.VMEM((256, 512), F32),
            pltpu.VMEM((256, 128), F32),
            pltpu.VMEM((128, 512), F32),
            pltpu.VMEM((128, 128), F32),
            pltpu.VMEM((1, 128), F32),
            pltpu.VMEM((TEN, 1, 128), F32),
            pltpu.VMEM((DP, 1, 128), F32),
            dma((8,)),
            dma((8,)),
            dma((8,)),
            dma((DP,)),
            dma((DP,)),
            dma((DP,)),
            dma((DP,)),
            dma((N_FORWARD,)),
            dma((DP, 4)),
            dma((TEN,)),
            dma((TEN,)),
            dma((4,)),
            dma((4,)),
            dma((N_FORWARD,)),
            dma((DP, 4)),
            dma((64,)),
            dma((DP, 4)),
            dma((TEN,)),
            dma((TEN,)),
            dma((DP,)),
            dma((DP,)),
        ],
        compiler_params=pltpu.CompilerParams(
            collective_id=0, has_side_effects=True, vmem_limit_bytes=60 * 1024 * 1024
        ),
    )(hidden, keys, vals, lens, ids, guid.reshape(2, 128), wq, kvw, wo, gain.reshape(1, 512), wh)


def solution(mesh):
    return jax.shard_map(
        body,
        mesh=mesh,
        in_specs=(
            P("stream", "tensor", "dp"),
            P("stream", "dp", "tensor", None, None),
            P("stream", "dp", "tensor", None, None),
            P("stream", "dp"),
            P(),
            P(),
            P("dp", "tensor"),
            P("dp", None, "tensor"),
            P("tensor", "dp"),
            P("dp"),
            P(None, ("dp", "tensor")),
        ),
        out_specs=P("stream", ("dp", "tensor")),
        check_vma=False,
    )
```

```python
import jax
import jax.numpy as jnp
from jax import lax
from jax.experimental import pallas as pl
from jax.experimental.pallas import tpu as pltpu
from jax.sharding import PartitionSpec as P

MESH = pl.DeviceIdType.MESH
F32 = jnp.float32
BF16 = jnp.bfloat16
WIDTH = 8192
HEAD = 128
RING = 4
DP = 16
TEN = 8

rope_theta = 500000.0
penalty_step = 1.5
norm_eps = 1e-05


MARKS = False
open_scope = []


def mark(name):
    if MARKS:
        if open_scope:
            open_scope.pop().__exit__(None, None, None)
        if name:
            open_scope.append(jax.named_scope(name))
            open_scope[0].__enter__()


def routes():
    found = []
    for depth in range(5):
        for dx in range(RING):
            for dy in range(RING):
                if min(dx, RING - dx) + min(dy, RING - dy) != depth:
                    continue
                for quarter in range(4):
                    first, second = (dx, dy) if quarter < 2 else (dy, dx)
                    names = ("x", "y") if quarter < 2 else ("y", "x")
                    odd = quarter % 2
                    hops = []
                    if second == 0:
                        if first == 0:
                            hops += [(names[0], 1), (names[0], -1)]
                        elif first == 1 and not odd:
                            hops += [(names[0], 1)]
                        elif first == 3 and odd:
                            hops += [(names[0], -1)]
                        hops += [(names[1], 1), (names[1], -1)]
                    elif second == 1 and not odd:
                        hops += [(names[1], 1)]
                    elif second == 3 and odd:
                        hops += [(names[1], -1)]
                    found.append((depth, dx, dy, quarter, hops))
    return found


ROUTES = routes()
N_FORWARD = sum(len(r[4]) for r in ROUTES)
OFFSETS = [
    sorted({(r[1], r[2]) for r in ROUTES if r[0] == depth}) for depth in range(5)
]


def kernel(
    hidden,
    keys,
    vals,
    lens,
    ids,
    guid,
    wq,
    kvw,
    wo,
    gain,
    wh,
    out,
    h_c,
    wq_v,
    kvw_v,
    k_v,
    v_v,
    wo_v,
    wh_v,
    ids_v,
    gain_all,
    part,
    recv_b,
    q_s,
    att_s,
    att_b,
    att_all,
    part_d,
    recv_d,
    resid,
    buf,
    acc,
    ssq,
    counts,
    gcol,
    tot_one,
    tot_t,
    tot_two,
    tot_d,
    load_sem,
    w_recv,
    f_recv,
    sib_recv,
    one,
):
    S = lax.axis_index("stream")
    D = lax.axis_index("dp")
    T = lax.axis_index("tensor")
    zl, c = T // 2, T % 2
    x, y = D // RING, D % RING
    sib = (S, D, zl * 2 + 1 - c)
    names = ("w", "a", "gain", "b", "c", "d", "z", "f", "sib", "t", "s")
    send_of = {name: one.at[n] for n, name in enumerate(names)}
    recv_of = {name: one.at[len(names) + n] for n, name in enumerate(names)}

    def remote(src, dst, ssem, rsem, dev):
        copy = pltpu.make_async_remote_copy(
            src_ref=src,
            dst_ref=dst,
            send_sem=ssem,
            recv_sem=rsem,
            device_id=dev,
            device_id_type=MESH,
        )
        copy.start()

    def arrived(ref, rsem):
        pltpu.make_async_remote_copy(
            src_ref=ref,
            dst_ref=ref,
            send_sem=send_of["w"],
            recv_sem=rsem,
            device_id=sib,
            device_id_type=MESH,
        ).wait_recv()

    def left(ref, name):
        pltpu.make_async_remote_copy(
            src_ref=ref,
            dst_ref=ref,
            send_sem=send_of[name],
            recv_sem=recv_of[name],
            device_id=sib,
            device_id_type=MESH,
        ).wait_send()

    mark("p00_entry")
    barrier = pltpu.get_barrier_semaphore()
    for i in range(1, DP):
        pl.semaphore_signal(
            barrier, inc=1, device_id=(S, (D + i) % DP, T), device_id_type=MESH
        )
        pl.semaphore_signal(
            barrier, inc=1, device_id=(S, (D + i) % DP, zl * 2 + 1 - c), device_id_type=MESH
        )
    for i in range(1, 16):
        other = (S * TEN + T + i) % 16
        pl.semaphore_signal(
            barrier, inc=1, device_id=(other // TEN, D, other % TEN), device_id_type=MESH
        )

    loads = []

    def load(src, dst, sem=None):
        copy = pltpu.make_async_copy(src, dst, load_sem.at[len(loads)] if sem is None else sem)
        copy.start()
        loads.append(copy)
        return copy

    load(hidden.at[0], h_c.at[zl], recv_of["a"])
    l_wq = load(wq, wq_v.at[c])
    l_kv = load(kvw, kvw_v.at[c])
    l_ids = load(ids.at[pl.ds(S * 128, 128), :], ids_v)
    l_k = load(keys.at[0, :, 0], k_v)
    l_v = load(vals.at[0, :, 0], v_v)
    l_wo = load(wo, wo_v.at[c])
    pl.semaphore_wait(barrier, 45)

    mark("p01_hidden")
    for dz in (3, 2, 1):
        dev = (S, D, ((zl + dz) % 4) * 2 + c)
        remote(hidden.at[0], h_c.at[zl], send_of["a"], recv_of["a"], dev)
    remote(wq, wq_v.at[c], send_of["w"], w_recv.at[0], sib)
    remote(kvw, kvw_v.at[c], send_of["w"], w_recv.at[1], sib)
    gain_all[D] = gain[...].astype(F32).reshape(1, 512)
    l_wh = load(wh, wh_v)
    remote(wo, wo_v.at[c], send_of["w"], w_recv.at[2], sib)
    l_wq.wait()
    l_kv.wait()
    arrived(h_c, recv_of["a"])

    mark("p02_qkv")
    h = h_c[...].reshape(128, 512)
    for i in range(2):
        g = (c + i) % 2
        if i == 1:
            arrived(wq_v.at[g], w_recv.at[0])
            arrived(kvw_v.at[g], w_recv.at[1])
        for n in range(4):
            cols = pl.ds(n * 256, 256)
            r = jnp.dot(h, wq_v[g, :, cols], preferred_element_type=F32)
            part[:, g, :, cols] = r.reshape(8, 16, 256).astype(BF16)
        for n in range(2):
            cols = pl.ds(1024 + n * 128, 128)
            r = jnp.dot(h, kvw_v[g, :, n, :], preferred_element_type=F32)
            part[:, g, :, cols] = r.reshape(8, 16, 128).astype(BF16)
        for n in range(8):
            k = (D // 2 + 1 + n) % 8
            to = 4 * (k // 2) + 2 * c + k % 2
            if i == 1:
                remote(
                    part.at[k, g], recv_b.at[D], send_of["b"], recv_of["b"], (S, to, zl * 2 + g)
                )
                continue

            @pl.when(to == D)
            def _():
                pltpu.make_async_copy(part.at[k, g], recv_b.at[D], recv_of["b"]).start()

            @pl.when(to != D)
            def _():
                remote(
                    part.at[k, g], recv_b.at[D], send_of["b"], recv_of["b"], (S, to, zl * 2 + g)
                )
    for i in range(1, DP):
        to = (D + i) % DP
        remote(gain_all.at[D], gain_all.at[D], send_of["gain"], recv_of["gain"], (S, to, T))

    mark("p03_tables")
    lane = lax.broadcasted_iota(jnp.int32, (16, HEAD), 1)
    row = lax.broadcasted_iota(jnp.int32, (16, HEAD), 0)
    freq = jnp.exp(((lane % 64).astype(F32) * (2.0 / HEAD)) * (-jnp.log(F32(rope_theta))))
    position = jnp.zeros((16, HEAD), jnp.int32)
    for p in range(16):
        position = jnp.where(row == p, lens[0, p], position)
    angle = position.astype(F32) * freq
    cosine = jnp.cos(angle)
    sine = jnp.sin(angle) * jnp.where(lane < 64, -1.0, 1.0)

    l_ids.wait()
    base = (D * TEN + T) * 512
    ids_v[...] = jnp.transpose(ids_v[...]) - base
    for n in range(4):
        column = lax.broadcasted_iota(jnp.int32, (128, 128), 0) + n * 128

        def add(r, total):
            for k in range(8):
                here = ids_v[pl.ds(r * 8 + k, 1), :]
                total = total + jnp.where(column == here, 1.0, 0.0)
            return total

        total = lax.fori_loop(0, 16, add, jnp.zeros((128, 128), F32))
        counts[:, pl.ds(n * 128, 128)] = jnp.transpose(total) * penalty_step
    gcol[...] = jnp.transpose(jnp.broadcast_to(guid[pl.ds(S, 1), :], (128, 128)))

    mark("p04_sumwait")
    arrived(recv_b, recv_of["b"])
    qkv = recv_b[0].astype(F32)
    for i in range(1, DP):
        qkv = qkv + recv_b[i].astype(F32)

    mark("p05_rope")

    def turn(v):
        return v * cosine + pltpu.roll(v, 64, 1) * sine

    for g in range(8):
        q_s[:, g, :] = turn(qkv[:, g * HEAD : (g + 1) * HEAD])
    k_new = turn(qkv[:, 1024:1152]).astype(BF16).astype(F32)
    v_new = qkv[:, 1152:1280].astype(BF16).astype(F32)

    mark("p06_attn")
    l_k.wait()
    l_v.wait()
    scale = HEAD ** (-0.5)
    slot_at = lax.broadcasted_iota(jnp.int32, (8, 256), 1)
    for start in (0, 8):
        prompts = range(start, start + 8)
        q = [q_s[p].astype(BF16) for p in prompts]
        scores = [
            lax.dot_general(
                q[p - start], k_v[p], (((1,), (1,)), ((), ())), preferred_element_type=F32
            )
            for p in prompts
        ]
        k_own = jnp.concatenate([jnp.broadcast_to(k_new[p : p + 1], (8, HEAD)) for p in prompts])
        v_own = jnp.concatenate([jnp.broadcast_to(v_new[p : p + 1], (8, HEAD)) for p in prompts])
        q_all = jnp.concatenate([v.astype(F32) for v in q])
        e_own = jnp.exp(jnp.sum(q_all * k_own, axis=1, keepdims=True) * scale)
        e = jnp.concatenate(
            [
                jnp.where(slot_at < lens[0, p], jnp.exp(scores[p - start] * scale), 0.0)
                for p in prompts
            ]
        )
        den = jnp.sum(e, axis=1, keepdims=True) + e_own
        w = (e / den).astype(BF16)
        w_own = (e_own / den).astype(BF16).astype(F32)
        o = jnp.concatenate(
            [
                jnp.dot(
                    w[(p - start) * 8 : (p - start + 1) * 8],
                    v_v[p],
                    preferred_element_type=F32,
                )
                for p in prompts
            ]
        )
        att_s[pl.ds(start, 8)] = (o + w_own * v_own).reshape(8, 8, HEAD)
    for g in range(8):
        att_b[:, pl.ds(g * HEAD, HEAD)] = att_s[:, g, :].astype(BF16)

    mark("p07_gatherC")
    core = (D // 2) % 2
    slot = c * 8 + 2 * (D // 4) + D % 2
    for i in range(1, DP):
        to = (D + i) % DP
        remote(att_b, att_all.at[slot], send_of["c"], recv_of["c"], (S, to, zl * 2 + core))

    @pl.when(core == c)
    def _():
        pltpu.make_async_copy(att_b, att_all.at[slot], recv_of["c"]).start()

    @pl.when(core != c)
    def _():
        remote(att_b, att_all.at[slot], send_of["c"], recv_of["c"], sib)

    l_wo.wait()
    arrived(wo_v.at[1 - c], w_recv.at[2])
    arrived(att_all, recv_of["c"])

    mark("p08_outproj")
    a0 = att_all[pl.ds(0, 8)].reshape(128, 1024)
    a1 = att_all[pl.ds(8, 8)].reshape(128, 1024)
    for n in range(2):
        cols = pl.ds(n * 256, 256)
        r = jnp.dot(a0, wo_v[0, :, cols], preferred_element_type=F32)
        r = r + jnp.dot(a1, wo_v[1, :, cols], preferred_element_type=F32)
        part_d[:, :, cols] = r.reshape(4, 32, 256).astype(BF16)

    def owned(z):
        inner = ((z + 1) // 2) % 2
        half = inner * S + (1 - inner) * (1 - S)
        return half, 2 * half + inner * (z - 1) + (1 - inner) * (z // 3)

    for dz in (3, 2, 1):
        to = (zl + dz) % 4
        block = owned(to)[1]
        remote(
            part_d.at[block],
            recv_d.at[3 - dz],
            send_of["d"],
            recv_of["d"],
            (S, D, to * 2 + c),
        )
    mark("p09_sumwaitD")
    my_half, mine = owned(zl)
    my_j = 2 * (mine % 2) + c
    total = h_c[mine].astype(F32) + part_d[mine].astype(F32)
    arrived(recv_d, recv_of["d"])
    for i in range(3):
        total = total + recv_d[i].astype(F32)
    resid[...] = total.astype(BF16)

    mark("p10_z")
    place = buf.at[S, D, pl.ds(my_j * 32, 32), :]
    for z in range(4):
        at_home = jnp.logical_and(my_half == S, 2 * z + S == T)

        @pl.when(at_home)
        def _():
            pltpu.make_async_copy(resid, place, recv_of["z"]).start()

        @pl.when(jnp.logical_not(at_home))
        def _():
            remote(resid, place, send_of["z"], recv_of["z"], (my_half, D, 2 * z + S))

    arrived(gain_all.at[pl.ds(0, DP - 1)], recv_of["gain"])
    l_wh.wait()
    acc[...] = jnp.zeros_like(acc)
    ssq[...] = jnp.zeros_like(ssq)

    def neighbour(name, step):
        if name == "x":
            return (S, ((x + RING + step) % RING) * RING + y, T)
        return (S, x * RING + (y + RING + step) % RING, T)

    def slot_of(dx, dy):
        return ((x + RING - dx) % RING) * RING + (y + RING - dy) % RING

    def pass_on(dx, dy):
        slot = slot_of(dx, dy)
        later = []
        for _, _, _, quarter, hops in [r for r in ROUTES if r[1:3] == (dx, dy)]:
            piece = buf.at[c, slot, pl.ds(quarter * 32, 32), :]
            sem = f_recv.at[slot, quarter]
            if (dx, dy) != (0, 0):
                arrived(piece, sem)
            else:
                later += [(piece, sem, hop) for hop in hops[2:]]
                hops = hops[:2]
            for hop in hops:
                remote(piece, piece, send_of["f"], sem, neighbour(*hop))
        for piece, sem, hop in later:
            remote(piece, piece, send_of["f"], sem, neighbour(*hop))
        whole = buf.at[c, slot]
        remote(whole, whole, send_of["sib"], sib_recv.at[slot], sib)

    def head(dx, dy):
        slot = slot_of(dx, dy)
        arrived(buf.at[1 - c, slot], sib_recv.at[slot])
        v = buf[:, slot].reshape(256, 512).astype(F32)
        v2 = v * v
        ssq[...] += v2[:, 0:128] + v2[:, 128:256] + v2[:, 256:384] + v2[:, 384:512]
        w = (v * gain_all[slot]).astype(BF16)
        acc[...] += jnp.dot(
            w,
            wh_v[pl.ds(pl.multiple_of(slot * 512, 512), 512), :],
            preferred_element_type=F32,
        )

    mark("p10b_zwait")
    arrived(buf.at[c, D], recv_of["z"])
    order = [offset for level in OFFSETS for offset in level]
    for n, offset in enumerate(order):
        mark(f"p11_gatherF{n:02d}")
        pass_on(*offset)
        if n >= 2:
            mark(f"p12_head{n-2:02d}")
            head(*order[n - 2])
    mark("p13_head14")
    head(*order[14])
    mark("p13_head15")
    head(*order[15])

    mark("p16_guided")
    inv = lax.rsqrt(jnp.sum(ssq[...], axis=1, keepdims=True) / WIDTH + norm_eps)
    cond = acc[0:128, :] * inv[0:128]
    uncond = acc[128:256, :] * inv[128:256]
    guide = gcol[:, 0:1]
    guided = uncond + guide * (cond - uncond) - counts[...]
    acc[0:128, :] = guided
    e = jnp.exp(guided)
    e = e[:, 0:128] + e[:, 128:256] + e[:, 256:384] + e[:, 384:512]
    mark("p17_total_t")
    tot_one[...] = jnp.sum(jnp.transpose(e), axis=0, keepdims=True)
    for i in range(1, TEN):
        to = (T + i) % TEN
        remote(tot_one, tot_t.at[i - 1], send_of["t"], recv_of["t"], (S, D, to))
    arrived(tot_t, recv_of["t"])
    mark("p18_total_d")
    tot_two[...] = tot_one[...] + jnp.sum(tot_t[...], axis=0)
    for i in range(1, DP):
        to = (D + i) % DP
        remote(tot_two, tot_d.at[i - 1], send_of["s"], recv_of["s"], (S, to, T))
    arrived(tot_d, recv_of["s"])
    totals = tot_two[...] + jnp.sum(tot_d[...], axis=0)
    log_total = jnp.transpose(jnp.broadcast_to(jnp.log(totals), (128, 128)))
    for n in range(4):
        cols = pl.ds(n * 128, 128)
        out[:, cols] = acc[0:128, cols] - log_total

    mark("p19_waitsend")
    left(wq_v.at[0], "w")
    left(kvw_v.at[0], "w")
    left(wo_v.at[0], "w")
    left(h_c.at[pl.ds(0, 3)], "a")
    left(gain_all.at[pl.ds(0, DP - 1)], "gain")
    left(part_d.at[pl.ds(0, 3)], "d")
    left(buf.at[0, pl.ds(0, 15)], "f")
    left(buf.at[0], "sib")
    left(tot_t, "t")
    left(tot_d, "s")
    kept_c = core == c
    kept_z = jnp.logical_and(my_half == S, c == S)

    @pl.when(kept_c)
    def _():
        left(recv_b.at[pl.ds(0, DP - 1)], "b")
        left(att_all.at[pl.ds(0, DP - 1)], "c")

    @pl.when(jnp.logical_not(kept_c))
    def _():
        left(recv_b, "b")
        left(att_all, "c")

    @pl.when(kept_z)
    def _():
        left(part_d.at[pl.ds(0, 3)], "z")

    @pl.when(jnp.logical_not(kept_z))
    def _():
        left(part_d, "z")

    mark(None)


def body(hidden, keys, vals, lens, ids, guid, wq, kvw, wo, gain, wh):
    dma = pltpu.SemaphoreType.DMA
    anywhere = pl.BlockSpec(memory_space=pl.ANY)
    vmem = pl.BlockSpec(memory_space=pltpu.VMEM)
    smem = pl.BlockSpec(memory_space=pltpu.SMEM)
    return pl.pallas_call(
        kernel,
        out_shape=jax.ShapeDtypeStruct((128, 512), F32),
        in_specs=[
            anywhere,
            anywhere,
            anywhere,
            smem,
            anywhere,
            vmem,
            anywhere,
            anywhere,
            anywhere,
            vmem,
            anywhere,
        ],
        out_specs=vmem,
        scratch_shapes=[
            pltpu.VMEM((4, 32, 512), BF16),
            pltpu.VMEM((2, 512, 1024), BF16),
            pltpu.VMEM((2, 512, 2, 128), BF16),
            pltpu.VMEM((16, 256, 128), BF16),
            pltpu.VMEM((16, 256, 128), BF16),
            pltpu.VMEM((2, 1024, 512), BF16),
            pltpu.VMEM((8192, 512), BF16),
            pltpu.VMEM((128, 128), jnp.int32),
            pltpu.VMEM((DP, 1, 512), F32),
            pltpu.VMEM((8, 2, 16, 1280), BF16),
            pltpu.VMEM((DP, 16, 1280), BF16),
            pltpu.VMEM((16, 8, 128), F32),
            pltpu.VMEM((16, 8, 128), F32),
            pltpu.VMEM((16, 1024), BF16),
            pltpu.VMEM((DP, 16, 1024), BF16),
            pltpu.VMEM((4, 32, 512), BF16),
            pltpu.VMEM((3, 32, 512), BF16),
            pltpu.VMEM((32, 512), BF16),
            pltpu.VMEM((2, DP, 128, 512), BF16),
            pltpu.VMEM((256, 512), F32),
            pltpu.VMEM((256, 128), F32),
            pltpu.VMEM((128, 512), F32),
            pltpu.VMEM((128, 128), F32),
            pltpu.VMEM((1, 128), F32),
            pltpu.VMEM((TEN - 1, 1, 128), F32),
            pltpu.VMEM((1, 128), F32),
            pltpu.VMEM((DP - 1, 1, 128), F32),
            dma((9,)),
            dma((3,)),
            dma((DP, 4)),
            dma((DP,)),
            dma((22,)),
        ],
        compiler_params=pltpu.CompilerParams(
            collective_id=0, has_side_effects=True, vmem_limit_bytes=60 * 1024 * 1024
        ),
    )(hidden, keys, vals, lens, ids, guid.reshape(2, 128), wq, kvw, wo, gain, wh)


def solution(mesh):
    return jax.shard_map(
        body,
        mesh=mesh,
        in_specs=(
            P("stream", "tensor", "dp"),
            P("stream", "dp", "tensor", None, None),
            P("stream", "dp", "tensor", None, None),
            P("stream", "dp"),
            P(),
            P(),
            P("dp", "tensor"),
            P("dp", None, "tensor"),
            P("tensor", "dp"),
            P("dp"),
            P(None, ("dp", "tensor")),
        ),
        out_specs=P("stream", ("dp", "tensor")),
        check_vma=False,
    )
```

```python
import heapq

import jax
import jax.numpy as jnp
from jax import lax
from jax.experimental import pallas as pl
from jax.experimental.pallas import tpu as pltpu
from jax.sharding import PartitionSpec as P

MESH = pl.DeviceIdType.MESH
F32 = jnp.float32
BF16 = jnp.bfloat16
WIDTH = 8192
HEAD = 128
RING = 4
DP = 16
TEN = 8

rope_theta = 500000.0
penalty_step = 1.5
norm_eps = 1e-05


MARKS = False
open_scope = []


def mark(name):
    if MARKS:
        if open_scope:
            open_scope.pop().__exit__(None, None, None)
        if name:
            open_scope.append(jax.named_scope(name))
            open_scope[0].__enter__()


def routes():
    found = []
    for depth in range(5):
        for dx in range(RING):
            for dy in range(RING):
                if min(dx, RING - dx) + min(dy, RING - dy) != depth:
                    continue
                for quarter in range(4):
                    first, second = (dx, dy) if quarter < 2 else (dy, dx)
                    names = ("x", "y") if quarter < 2 else ("y", "x")
                    odd = quarter % 2
                    hops = []
                    if second == 0:
                        if first == 0:
                            hops += [(names[0], 1), (names[0], -1)]
                        elif first == 1 and not odd:
                            hops += [(names[0], 1)]
                        elif first == 3 and odd:
                            hops += [(names[0], -1)]
                        hops += [(names[1], 1), (names[1], -1)]
                    elif second == 1 and not odd:
                        hops += [(names[1], 1)]
                    elif second == 3 and odd:
                        hops += [(names[1], -1)]
                    found.append((depth, dx, dy, quarter, hops))
    return found


HOPS = {r[1:4]: r[4] for r in routes()}
N_FORWARD = sum(len(hops) for hops in HOPS.values())
PLACE = [4 * (g // 4) + 2 * (g % 2) + (g // 2) % 2 for g in range(8)]


def onward(piece, hop):
    dx, dy, quarter = piece
    axis, step = hop
    if axis == "x":
        return (dx + step) % RING, dy, quarter
    return dx, (dy + step) % RING, quarter


def further(piece):
    return max([1 + further(onward(piece, hop)) for hop in HOPS[piece]], default=0)


def forwards(piece):
    return sorted(HOPS[piece], key=lambda hop: -further(onward(piece, hop)))


def plan():
    free, arrivals, order = {}, [], []

    def send(piece, hop, now):
        free[hop] = max(free.get(hop, 0.0), now) + 0.7
        heapq.heappush(arrivals, (free[hop] + 1.66, len(order), onward(piece, hop)))

    own = [(0, 0, quarter) for quarter in range(4)]
    first = [(piece, hop) for piece in own for hop in HOPS[piece][:2]]
    first += [(piece, hop) for piece in own for hop in HOPS[piece][2:]]
    for piece, hop in first:
        send(piece, hop, 0.0)
    now = 0.0
    while arrivals:
        when, _, piece = heapq.heappop(arrivals)
        now = max(now, when) + 0.02
        order.append(piece)
        for hop in forwards(piece):
            send(piece, hop, now)
    return order


ORDER = plan()


def kernel(
    hidden,
    keys,
    vals,
    lens,
    ids,
    guid,
    wq,
    kvw,
    wo,
    gain,
    wh,
    out,
    h_c,
    wq_v,
    kvw_v,
    k_v,
    v_v,
    wo_v,
    wh_v,
    ids_v,
    gain_all,
    part,
    recv_b,
    q_s,
    att_s,
    att_b,
    att_all,
    part_d,
    recv_d,
    resid,
    buf,
    acc,
    ssq,
    counts,
    gcol,
    tot_one,
    tot_all,
    load_sem,
    w_recv,
    z_recv,
    f_recv,
    sib_recv,
    one,
):
    S = lax.axis_index("stream")
    D = lax.axis_index("dp")
    T = lax.axis_index("tensor")
    zl, c = T // 2, T % 2
    x, y = D // RING, D % RING
    sib = (S, D, zl * 2 + 1 - c)
    names = ("w", "a", "gain", "b", "c", "d", "z", "f", "sib", "t")
    send_of = {name: one.at[n] for n, name in enumerate(names)}
    recv_of = {name: one.at[len(names) + n] for n, name in enumerate(names)}

    def remote(src, dst, ssem, rsem, dev):
        copy = pltpu.make_async_remote_copy(
            src_ref=src,
            dst_ref=dst,
            send_sem=ssem,
            recv_sem=rsem,
            device_id=dev,
            device_id_type=MESH,
        )
        copy.start()

    def arrived(ref, rsem):
        pltpu.make_async_remote_copy(
            src_ref=ref,
            dst_ref=ref,
            send_sem=send_of["w"],
            recv_sem=rsem,
            device_id=sib,
            device_id_type=MESH,
        ).wait_recv()

    def left(ref, name):
        pltpu.make_async_remote_copy(
            src_ref=ref,
            dst_ref=ref,
            send_sem=send_of[name],
            recv_sem=recv_of[name],
            device_id=sib,
            device_id_type=MESH,
        ).wait_send()

    mark("p00_entry")
    barrier = pltpu.get_barrier_semaphore()
    for i in range(1, DP):
        pl.semaphore_signal(
            barrier, inc=1, device_id=(S, (D + i) % DP, T), device_id_type=MESH
        )
        pl.semaphore_signal(
            barrier, inc=1, device_id=(S, (D + i) % DP, zl * 2 + 1 - c), device_id_type=MESH
        )
    for i in range(1, 16):
        other = (S * TEN + T + i) % 16
        pl.semaphore_signal(
            barrier, inc=1, device_id=(other // TEN, D, other % TEN), device_id_type=MESH
        )

    loads = []

    def load(src, dst, sem=None):
        if sem is None:
            sem = load_sem.at[len(loads)]
            loads.append(sem)
        copy = pltpu.make_async_copy(src, dst, sem)
        copy.start()
        return copy

    load(hidden.at[0, pl.ds(c * 16, 16)], h_c.at[T], recv_of["a"])
    l_wq = load(wq, wq_v.at[c])
    l_kv = load(kvw, kvw_v.at[c])
    for g in range(8):
        load(
            ids.at[pl.ds(S * 128 + PLACE[g] * 16, 16), :],
            ids_v.at[pl.ds(g * 16, 16), :],
            load_sem.at[8],
        )
    l_k = load(keys.at[0, :, 0], k_v)
    l_v = load(vals.at[0, :, 0], v_v)
    l_wo = load(wo, wo_v.at[c])
    pl.semaphore_wait(barrier, 45)

    mark("p01_hidden")
    for dz in (3, 2, 1):
        for core in (0, 1):
            dev = (S, D, ((zl + dz) % 4) * 2 + core)
            remote(
                hidden.at[0, pl.ds(core * 16, 16)], h_c.at[T], send_of["a"], recv_of["a"], dev
            )
    remote(hidden.at[0, pl.ds(16 - c * 16, 16)], h_c.at[T], send_of["a"], recv_of["a"], sib)
    remote(wq, wq_v.at[c], send_of["w"], w_recv.at[0], sib)
    remote(kvw, kvw_v.at[c], send_of["w"], w_recv.at[1], sib)
    gain_all[D] = gain[...].astype(F32).reshape(1, 512)
    l_wh = load(wh, wh_v)
    remote(wo, wo_v.at[c], send_of["w"], w_recv.at[2], sib)
    l_wq.wait()
    l_kv.wait()
    arrived(h_c, recv_of["a"])

    mark("p02_qkv")
    h = h_c[...].reshape(128, 512)
    for i in range(2):
        g = (c + i) % 2
        if i == 1:
            arrived(wq_v.at[g], w_recv.at[0])
            arrived(kvw_v.at[g], w_recv.at[1])
        for n in range(4):
            cols = pl.ds(n * 256, 256)
            r = jnp.dot(h, wq_v[g, :, cols], preferred_element_type=F32)
            part[:, g, :, cols] = r.reshape(8, 16, 256).astype(BF16)
        for n in range(2):
            cols = pl.ds(1024 + n * 128, 128)
            r = jnp.dot(h, kvw_v[g, :, n, :], preferred_element_type=F32)
            part[:, g, :, cols] = r.reshape(8, 16, 128).astype(BF16)
        for n in range(8):
            k = (D // 2 + 1 + n) % 8
            to = 2 * k + c
            if i == 1:
                remote(
                    part.at[k, g], recv_b.at[D], send_of["b"], recv_of["b"], (S, to, zl * 2 + g)
                )
                continue

            @pl.when(to == D)
            def _():
                pltpu.make_async_copy(part.at[k, g], recv_b.at[D], recv_of["b"]).start()

            @pl.when(to != D)
            def _():
                remote(
                    part.at[k, g], recv_b.at[D], send_of["b"], recv_of["b"], (S, to, zl * 2 + g)
                )
    for i in range(1, DP):
        to = (D + i) % DP
        remote(gain_all.at[D], gain_all.at[D], send_of["gain"], recv_of["gain"], (S, to, T))

    mark("p03_tables")
    lane = lax.broadcasted_iota(jnp.int32, (16, HEAD), 1)
    row = lax.broadcasted_iota(jnp.int32, (16, HEAD), 0)
    freq = jnp.exp(((lane % 64).astype(F32) * (2.0 / HEAD)) * (-jnp.log(F32(rope_theta))))
    position = jnp.zeros((16, HEAD), jnp.int32)
    for p in range(16):
        position = jnp.where(row == p, lens[0, p], position)
    angle = position.astype(F32) * freq
    cosine = jnp.cos(angle)
    sine = jnp.sin(angle) * jnp.where(lane < 64, -1.0, 1.0)

    pltpu.make_async_copy(ids.at[pl.ds(0, 128), :], ids_v, load_sem.at[8]).wait()
    base = (D * TEN + T) * 512
    ids_v[...] = jnp.transpose(ids_v[...]) - base
    for n in range(4):
        column = lax.broadcasted_iota(jnp.int32, (128, 128), 0) + n * 128

        def add(r, total):
            for k in range(8):
                here = ids_v[pl.ds(r * 8 + k, 1), :]
                total = total + jnp.where(column == here, 1.0, 0.0)
            return total

        total = lax.fori_loop(0, 16, add, jnp.zeros((128, 128), F32))
        counts[:, pl.ds(n * 128, 128)] = jnp.transpose(total) * penalty_step
    guide = jnp.transpose(jnp.broadcast_to(guid[pl.ds(S, 1), :], (128, 128)))
    for g in range(8):
        gcol[g * 16 : (g + 1) * 16] = guide[PLACE[g] * 16 : (PLACE[g] + 1) * 16]

    mark("p04_sumwait")
    arrived(recv_b, recv_of["b"])
    qkv = recv_b[0].astype(F32)
    for i in range(1, DP):
        qkv = qkv + recv_b[i].astype(F32)

    mark("p05_rope")

    def turn(v):
        return v * cosine + pltpu.roll(v, 64, 1) * sine

    for g in range(8):
        q_s[:, g, :] = turn(qkv[:, g * HEAD : (g + 1) * HEAD])
    k_new = turn(qkv[:, 1024:1152]).astype(BF16).astype(F32)
    v_new = qkv[:, 1152:1280].astype(BF16).astype(F32)

    mark("p06_attn")
    l_k.wait()
    l_v.wait()
    scale = HEAD ** (-0.5)
    slot_at = lax.broadcasted_iota(jnp.int32, (8, 256), 1)
    for start in (0, 8):
        prompts = range(start, start + 8)
        q = [q_s[p].astype(BF16) for p in prompts]
        scores = [
            lax.dot_general(
                q[p - start], k_v[p], (((1,), (1,)), ((), ())), preferred_element_type=F32
            )
            for p in prompts
        ]
        k_own = jnp.concatenate([jnp.broadcast_to(k_new[p : p + 1], (8, HEAD)) for p in prompts])
        v_own = jnp.concatenate([jnp.broadcast_to(v_new[p : p + 1], (8, HEAD)) for p in prompts])
        q_all = jnp.concatenate([v.astype(F32) for v in q])
        e_own = jnp.exp(jnp.sum(q_all * k_own, axis=1, keepdims=True) * scale)
        e = jnp.concatenate(
            [
                jnp.where(slot_at < lens[0, p], jnp.exp(scores[p - start] * scale), 0.0)
                for p in prompts
            ]
        )
        den = jnp.sum(e, axis=1, keepdims=True) + e_own
        w = (e / den).astype(BF16)
        w_own = (e_own / den).astype(BF16).astype(F32)
        o = jnp.concatenate(
            [
                jnp.dot(
                    w[(p - start) * 8 : (p - start + 1) * 8],
                    v_v[p],
                    preferred_element_type=F32,
                )
                for p in prompts
            ]
        )
        att_s[pl.ds(start, 8)] = (o + w_own * v_own).reshape(8, 8, HEAD)
    for g in range(8):
        att_b[:, pl.ds(g * HEAD, HEAD)] = att_s[:, g, :].astype(BF16)

    mark("p07_gatherC")
    core = D % 2
    slot = c * 8 + D // 2
    for i in range(1, DP):
        to = (D + i) % DP
        remote(att_b, att_all.at[slot], send_of["c"], recv_of["c"], (S, to, zl * 2 + core))

    @pl.when(core == c)
    def _():
        pltpu.make_async_copy(att_b, att_all.at[slot], recv_of["c"]).start()

    @pl.when(core != c)
    def _():
        remote(att_b, att_all.at[slot], send_of["c"], recv_of["c"], sib)

    l_wo.wait()
    arrived(wo_v.at[1 - c], w_recv.at[2])
    arrived(att_all, recv_of["c"])

    mark("p08_outproj")
    a0 = att_all[pl.ds(0, 8)].reshape(128, 1024)
    a1 = att_all[pl.ds(8, 8)].reshape(128, 1024)
    for n in range(2):
        cols = pl.ds(n * 256, 256)
        r = jnp.dot(a0, wo_v[0, :, cols], preferred_element_type=F32)
        r = r + jnp.dot(a1, wo_v[1, :, cols], preferred_element_type=F32)
        part_d[:, :, cols] = r.reshape(4, 32, 256).astype(BF16)

    def owned(z):
        inner = ((z + 1) // 2) % 2
        half = inner * S + (1 - inner) * (1 - S)
        return half, 2 * half + inner * (z - 1) + (1 - inner) * (z // 3)

    for dz in (3, 2, 1):
        to = (zl + dz) % 4
        block = owned(to)[1]
        remote(
            part_d.at[block],
            recv_d.at[3 - dz],
            send_of["d"],
            recv_of["d"],
            (S, D, to * 2 + c),
        )
    mark("p09_sumwaitD")
    my_half, mine = owned(zl)
    my_j = 2 * (mine % 2) + c
    total = h_c[pl.ds(2 * mine, 2)].reshape(32, 512).astype(F32) + part_d[mine].astype(F32)
    arrived(recv_d, recv_of["d"])
    for i in range(3):
        total = total + recv_d[i].astype(F32)
    resid[...] = total.astype(BF16)

    mark("p10_z")
    place = buf.at[S, D, pl.ds(my_j * 32, 32), :]
    for z in range(4):
        at_home = jnp.logical_and(my_half == S, 2 * z + S == T)

        @pl.when(at_home)
        def _():
            pltpu.make_async_copy(resid, place, z_recv.at[my_j]).start()

        @pl.when(jnp.logical_not(at_home))
        def _():
            remote(resid, place, send_of["z"], z_recv.at[my_j], (my_half, D, 2 * z + S))

    arrived(gain_all.at[pl.ds(0, DP - 1)], recv_of["gain"])
    l_wh.wait()
    acc[...] = jnp.zeros_like(acc)
    ssq[...] = jnp.zeros_like(ssq)

    def neighbour(name, step):
        if name == "x":
            return (S, ((x + RING + step) % RING) * RING + y, T)
        return (S, x * RING + (y + RING + step) % RING, T)

    def slot_of(dx, dy):
        return ((x + RING - dx) % RING) * RING + (y + RING - dy) % RING

    def send_on(piece, hops):
        slot, quarter = slot_of(*piece[:2]), piece[2]
        rows = buf.at[c, slot, pl.ds(quarter * 32, 32), :]
        for hop in hops:
            remote(rows, rows, send_of["f"], f_recv.at[slot, quarter], neighbour(*hop))

    def share(dx, dy):
        whole = buf.at[c, slot_of(dx, dy)]
        remote(whole, whole, send_of["sib"], sib_recv.at[slot_of(dx, dy)], sib)

    def head(dx, dy):
        slot = slot_of(dx, dy)
        arrived(buf.at[1 - c, slot], sib_recv.at[slot])
        v = buf[:, slot].reshape(256, 512).astype(F32)
        v2 = v * v
        ssq[...] += v2[:, 0:128] + v2[:, 128:256] + v2[:, 256:384] + v2[:, 384:512]
        w = (v * gain_all[slot]).astype(BF16)
        acc[...] += jnp.dot(
            w,
            wh_v[pl.ds(pl.multiple_of(slot * 512, 512), 512), :],
            preferred_element_type=F32,
        )

    mark("p10b_zwait")
    for quarter in range(4):
        arrived(buf.at[c, D, pl.ds(quarter * 32, 32), :], z_recv.at[quarter])
        send_on((0, 0, quarter), HOPS[(0, 0, quarter)][:2])
    mark("p11_own")
    for quarter in range(4):
        send_on((0, 0, quarter), HOPS[(0, 0, quarter)][2:])
    share(0, 0)
    complete = [(0, (0, 0))]
    held = {}
    for n, piece in enumerate(ORDER):
        if n % 10 == 0:
            mark(f"p12_pieces{n:02d}")
        dx, dy, quarter = piece
        slot = slot_of(dx, dy)
        arrived(buf.at[c, slot, pl.ds(quarter * 32, 32), :], f_recv.at[slot, quarter])
        send_on(piece, forwards(piece))
        held[dx, dy] = held.get((dx, dy), 0) + 1
        if held[dx, dy] == 4:
            share(dx, dy)
            complete.append((n, (dx, dy)))
        if complete and n - complete[0][0] >= 8:
            head(*complete.pop(0)[1])
    mark("p13_lastheads")
    for _, offset in complete:
        head(*offset)

    mark("p16_guided")
    inv = lax.rsqrt(jnp.sum(ssq[...], axis=1, keepdims=True) / WIDTH + norm_eps)
    cond = acc[0:128, :] * inv[0:128]
    uncond = acc[128:256, :] * inv[128:256]
    guide = gcol[:, 0:1]
    guided = uncond + guide * (cond - uncond) - counts[...]
    acc[0:128, :] = guided
    e = jnp.exp(guided)
    e = e[:, 0:128] + e[:, 128:256] + e[:, 256:384] + e[:, 384:512]
    mark("p17_total")
    tot_one[...] = jnp.sum(jnp.transpose(e), axis=0, keepdims=True)

    def tell(i, carry):
        to = (D * TEN + T + i) % (DP * TEN)
        remote(
            tot_one, tot_all.at[i - 1], send_of["t"], recv_of["t"], (S, to // TEN, to % TEN)
        )
        return carry

    lax.fori_loop(1, DP * TEN, tell, 0)
    arrived(tot_all, recv_of["t"])
    mark("p18_out")
    totals = tot_one[...] + jnp.sum(tot_all[...], axis=0)
    log_total = jnp.transpose(jnp.broadcast_to(jnp.log(totals), (128, 128)))
    for g in range(8):
        for n in range(4):
            cols = pl.ds(n * 128, 128)
            out[pl.ds(PLACE[g] * 16, 16), cols] = (
                acc[pl.ds(g * 16, 16), cols] - log_total[g * 16 : (g + 1) * 16]
            )

    mark("p19_waitsend")
    left(wq_v.at[0], "w")
    left(kvw_v.at[0], "w")
    left(wo_v.at[0], "w")
    left(h_c.at[pl.ds(0, 7)], "a")
    left(gain_all.at[pl.ds(0, DP - 1)], "gain")
    left(part_d.at[pl.ds(0, 3)], "d")
    left(buf.at[0, pl.ds(0, 15)], "f")
    left(buf.at[0], "sib")
    left(tot_all, "t")
    kept_c = core == c
    kept_z = jnp.logical_and(my_half == S, c == S)

    @pl.when(kept_c)
    def _():
        left(recv_b.at[pl.ds(0, DP - 1)], "b")
        left(att_all.at[pl.ds(0, DP - 1)], "c")

    @pl.when(jnp.logical_not(kept_c))
    def _():
        left(recv_b, "b")
        left(att_all, "c")

    @pl.when(kept_z)
    def _():
        left(part_d.at[pl.ds(0, 3)], "z")

    @pl.when(jnp.logical_not(kept_z))
    def _():
        left(part_d, "z")

    mark(None)


def body(hidden, keys, vals, lens, ids, guid, wq, kvw, wo, gain, wh):
    dma = pltpu.SemaphoreType.DMA
    anywhere = pl.BlockSpec(memory_space=pl.ANY)
    vmem = pl.BlockSpec(memory_space=pltpu.VMEM)
    smem = pl.BlockSpec(memory_space=pltpu.SMEM)
    return pl.pallas_call(
        kernel,
        out_shape=jax.ShapeDtypeStruct((128, 512), F32),
        in_specs=[
            anywhere,
            anywhere,
            anywhere,
            smem,
            anywhere,
            vmem,
            anywhere,
            anywhere,
            anywhere,
            vmem,
            anywhere,
        ],
        out_specs=vmem,
        scratch_shapes=[
            pltpu.VMEM((TEN, 16, 512), BF16),
            pltpu.VMEM((2, 512, 1024), BF16),
            pltpu.VMEM((2, 512, 2, 128), BF16),
            pltpu.VMEM((16, 256, 128), BF16),
            pltpu.VMEM((16, 256, 128), BF16),
            pltpu.VMEM((2, 1024, 512), BF16),
            pltpu.VMEM((8192, 512), BF16),
            pltpu.VMEM((128, 128), jnp.int32),
            pltpu.VMEM((DP, 1, 512), F32),
            pltpu.VMEM((8, 2, 16, 1280), BF16),
            pltpu.VMEM((DP, 16, 1280), BF16),
            pltpu.VMEM((16, 8, 128), F32),
            pltpu.VMEM((16, 8, 128), F32),
            pltpu.VMEM((16, 1024), BF16),
            pltpu.VMEM((DP, 16, 1024), BF16),
            pltpu.VMEM((4, 32, 512), BF16),
            pltpu.VMEM((3, 32, 512), BF16),
            pltpu.VMEM((32, 512), BF16),
            pltpu.VMEM((2, DP, 128, 512), BF16),
            pltpu.VMEM((256, 512), F32),
            pltpu.VMEM((256, 128), F32),
            pltpu.VMEM((128, 512), F32),
            pltpu.VMEM((128, 128), F32),
            pltpu.VMEM((1, 128), F32),
            pltpu.VMEM((DP * TEN - 1, 1, 128), F32),
            dma((9,)),
            dma((3,)),
            dma((4,)),
            dma((DP, 4)),
            dma((DP,)),
            dma((20,)),
        ],
        compiler_params=pltpu.CompilerParams(
            collective_id=0, has_side_effects=True, vmem_limit_bytes=60 * 1024 * 1024
        ),
    )(hidden, keys, vals, lens, ids, guid.reshape(2, 128), wq, kvw, wo, gain, wh)


def solution(mesh):
    return jax.shard_map(
        body,
        mesh=mesh,
        in_specs=(
            P("stream", "tensor", "dp"),
            P("stream", "dp", "tensor", None, None),
            P("stream", "dp", "tensor", None, None),
            P("stream", "dp"),
            P(),
            P(),
            P("dp", "tensor"),
            P("dp", None, "tensor"),
            P("tensor", "dp"),
            P("dp"),
            P(None, ("dp", "tensor")),
        ),
        out_specs=P("stream", ("dp", "tensor")),
        check_vma=False,
    )
```

```python
import heapq

import jax
import jax.numpy as jnp
from jax import lax
from jax.experimental import pallas as pl
from jax.experimental.pallas import tpu as pltpu
from jax.sharding import PartitionSpec as P

MESH = pl.DeviceIdType.MESH
F32 = jnp.float32
BF16 = jnp.bfloat16
WIDTH = 8192
HEAD = 128
RING = 4
DP = 16
TEN = 8

rope_theta = 500000.0
penalty_step = 1.5
norm_eps = 1e-05


MARKS = False
open_scope = []


def mark(name):
    if MARKS:
        if open_scope:
            open_scope.pop().__exit__(None, None, None)
        if name:
            open_scope.append(jax.named_scope(name))
            open_scope[0].__enter__()


def routes():
    found = []
    for depth in range(5):
        for dx in range(RING):
            for dy in range(RING):
                if min(dx, RING - dx) + min(dy, RING - dy) != depth:
                    continue
                for quarter in range(4):
                    first, second = (dx, dy) if quarter < 2 else (dy, dx)
                    names = ("x", "y") if quarter < 2 else ("y", "x")
                    odd = quarter % 2
                    hops = []
                    if second == 0:
                        if first == 0:
                            hops += [(names[0], 1), (names[0], -1)]
                        elif first == 1 and not odd:
                            hops += [(names[0], 1)]
                        elif first == 3 and odd:
                            hops += [(names[0], -1)]
                        hops += [(names[1], 1), (names[1], -1)]
                    elif second == 1 and not odd:
                        hops += [(names[1], 1)]
                    elif second == 3 and odd:
                        hops += [(names[1], -1)]
                    found.append((depth, dx, dy, quarter, hops))
    return found


HOPS = {r[1:4]: r[4] for r in routes()}
N_FORWARD = sum(len(hops) for hops in HOPS.values())
PLACE = [4 * (g // 4) + 2 * (g % 2) + (g // 2) % 2 for g in range(8)]


def onward(piece, hop):
    dx, dy, quarter = piece
    axis, step = hop
    if axis == "x":
        return (dx + step) % RING, dy, quarter
    return dx, (dy + step) % RING, quarter


def further(piece):
    return max([1 + further(onward(piece, hop)) for hop in HOPS[piece]], default=0)


def forwards(piece):
    return sorted(HOPS[piece], key=lambda hop: -further(onward(piece, hop)))


def plan():
    free, arrivals, order = {}, [], []

    def send(piece, hop, now):
        free[hop] = max(free.get(hop, 0.0), now) + 0.7
        heapq.heappush(arrivals, (free[hop] + 1.66, len(order), onward(piece, hop)))

    own = [(0, 0, quarter) for quarter in range(4)]
    first = [(piece, hop) for piece in own for hop in HOPS[piece][:2]]
    first += [(piece, hop) for piece in own for hop in HOPS[piece][2:]]
    for piece, hop in first:
        send(piece, hop, 0.0)
    now = 0.0
    while arrivals:
        when, _, piece = heapq.heappop(arrivals)
        now = max(now, when) + 0.02
        order.append(piece)
        for hop in forwards(piece):
            send(piece, hop, now)
    return order


ORDER = plan()
FAR = (2, 1, 3, 0)
PLANE = sorted(
    [(dx, dy) for dx in range(RING) for dy in range(RING)],
    key=lambda o: -min(o[0], RING - o[0]) - min(o[1], RING - o[1]),
)


def kernel(
    hidden,
    keys,
    vals,
    lens,
    ids,
    guid,
    wq,
    kvw,
    wo,
    gain,
    wh,
    out,
    h_c,
    wq_v,
    kvw_v,
    kv_v,
    k_v,
    v_v,
    wo_v,
    wh_v,
    ids_v,
    gain_all,
    part,
    recv_b,
    q_s,
    att_s,
    att_b,
    att_all,
    part_d,
    recv_d,
    resid,
    buf,
    acc,
    ssq,
    counts,
    gcol,
    tot_one,
    tot_all,
    load_sem,
    w_recv,
    z_recv,
    c_recv,
    f_recv,
    sib_recv,
    one,
):
    S = lax.axis_index("stream")
    D = lax.axis_index("dp")
    T = lax.axis_index("tensor")
    zl, c = T // 2, T % 2
    x, y = D // RING, D % RING
    sib = (S, D, zl * 2 + 1 - c)
    names = ("w", "a", "gain", "b", "c", "d", "z", "f", "sib", "t")
    send_of = {name: one.at[n] for n, name in enumerate(names)}
    recv_of = {name: one.at[len(names) + n] for n, name in enumerate(names)}

    def remote(src, dst, ssem, rsem, dev):
        copy = pltpu.make_async_remote_copy(
            src_ref=src,
            dst_ref=dst,
            send_sem=ssem,
            recv_sem=rsem,
            device_id=dev,
            device_id_type=MESH,
        )
        copy.start()

    def arrived(ref, rsem):
        pltpu.make_async_remote_copy(
            src_ref=ref,
            dst_ref=ref,
            send_sem=send_of["w"],
            recv_sem=rsem,
            device_id=sib,
            device_id_type=MESH,
        ).wait_recv()

    def left(ref, name):
        pltpu.make_async_remote_copy(
            src_ref=ref,
            dst_ref=ref,
            send_sem=send_of[name],
            recv_sem=recv_of[name],
            device_id=sib,
            device_id_type=MESH,
        ).wait_send()

    def peer(dx, dy):
        return ((x + dx) % RING) * RING + (y + dy) % RING

    mark("p00_entry")
    barrier = pltpu.get_barrier_semaphore()
    for i in range(1, DP):
        pl.semaphore_signal(
            barrier, inc=1, device_id=(S, (D + i) % DP, T), device_id_type=MESH
        )
        pl.semaphore_signal(
            barrier, inc=1, device_id=(S, (D + i) % DP, zl * 2 + 1 - c), device_id_type=MESH
        )
    for i in range(1, 16):
        other = (S * TEN + T + i) % 16
        pl.semaphore_signal(
            barrier, inc=1, device_id=(other // TEN, D, other % TEN), device_id_type=MESH
        )

    loads = []

    def load(src, dst, sem=None):
        if sem is None:
            sem = load_sem.at[len(loads)]
            loads.append(sem)
        copy = pltpu.make_async_copy(src, dst, sem)
        copy.start()
        return copy

    load(hidden.at[0, pl.ds(c * 16, 16)], h_c.at[T], recv_of["a"])
    l_wq = load(wq, wq_v.at[c])
    l_kv = load(kvw, kvw_v)
    for g in range(8):
        load(
            ids.at[pl.ds(S * 128 + PLACE[g] * 16, 16), :],
            ids_v.at[pl.ds(g * 16, 16), :],
            load_sem.at[8],
        )
    l_k = load(keys.at[0, :, 0], k_v)
    l_v = load(vals.at[0, :, 0], v_v)
    l_wo = load(wo, wo_v.at[c])
    pl.semaphore_wait(barrier, 45)

    mark("p01_hidden")
    for dz in (3, 2, 1):
        for core in (0, 1):
            dev = (S, D, ((zl + dz) % 4) * 2 + core)
            remote(
                hidden.at[0, pl.ds(core * 16, 16)], h_c.at[T], send_of["a"], recv_of["a"], dev
            )
    remote(hidden.at[0, pl.ds(16 - c * 16, 16)], h_c.at[T], send_of["a"], recv_of["a"], sib)
    remote(wq, wq_v.at[c], send_of["w"], w_recv.at[0], sib)
    gain_all[D] = gain[...].astype(F32).reshape(1, 512)
    l_wh = load(wh, wh_v)
    remote(wo, wo_v.at[c], send_of["w"], w_recv.at[2], sib)
    l_kv.wait()
    for n in range(2):
        kv_v[c, :, n * 128 : (n + 1) * 128] = kvw_v[:, n, :]
    l_wq.wait()
    remote(kv_v.at[c], kv_v.at[c], send_of["w"], w_recv.at[1], sib)
    arrived(h_c, recv_of["a"])

    mark("p02_qkv")
    h = h_c[...].reshape(128, 512)
    for i in range(2):
        g = (c + i) % 2
        if i == 1:
            arrived(wq_v.at[g], w_recv.at[0])
            arrived(kv_v.at[g], w_recv.at[1])
        for n in range(4):
            cols = pl.ds(n * 256, 256)
            r = jnp.dot(h, wq_v[g, :, cols], preferred_element_type=F32)
            part[:, g, :, cols] = r.reshape(8, 16, 256).astype(BF16)
        r = jnp.dot(h, kv_v[g], preferred_element_type=F32)
        part[:, g, :, pl.ds(1024, 256)] = r.reshape(8, 16, 256).astype(BF16)
        for n in range(8):
            to = peer(FAR[n // 2], (y + c) % 2 + 2 - 2 * (n % 2))
            k = to // 2
            if i == 1:
                remote(
                    part.at[k, g], recv_b.at[D], send_of["b"], recv_of["b"], (S, to, zl * 2 + g)
                )
                continue

            @pl.when(to == D)
            def _():
                pltpu.make_async_copy(part.at[k, g], recv_b.at[D], recv_of["b"]).start()

            @pl.when(to != D)
            def _():
                remote(
                    part.at[k, g], recv_b.at[D], send_of["b"], recv_of["b"], (S, to, zl * 2 + g)
                )
    for i in range(1, DP):
        to = (D + i) % DP
        remote(gain_all.at[D], gain_all.at[D], send_of["gain"], recv_of["gain"], (S, to, T))

    mark("p03_tables")
    lane = lax.broadcasted_iota(jnp.int32, (16, HEAD), 1)
    row = lax.broadcasted_iota(jnp.int32, (16, HEAD), 0)
    freq = jnp.exp(((lane % 64).astype(F32) * (2.0 / HEAD)) * (-jnp.log(F32(rope_theta))))
    position = jnp.zeros((16, HEAD), jnp.int32)
    for p in range(16):
        position = jnp.where(row == p, lens[0, p], position)
    angle = position.astype(F32) * freq
    cosine = jnp.cos(angle)
    sine = jnp.sin(angle) * jnp.where(lane < 64, -1.0, 1.0)

    pltpu.make_async_copy(ids.at[pl.ds(0, 128), :], ids_v, load_sem.at[8]).wait()
    base = (D * TEN + T) * 512
    ids_v[...] = jnp.transpose(ids_v[...]) - base
    for n in range(4):
        column = lax.broadcasted_iota(jnp.int32, (128, 128), 0) + n * 128

        def add(r, total):
            for k in range(8):
                here = ids_v[pl.ds(r * 8 + k, 1), :]
                total = total + jnp.where(column == here, 1.0, 0.0)
            return total

        total = lax.fori_loop(0, 16, add, jnp.zeros((128, 128), F32))
        counts[:, pl.ds(n * 128, 128)] = jnp.transpose(total) * penalty_step
    guide = jnp.transpose(jnp.broadcast_to(guid[pl.ds(S, 1), :], (128, 128)))
    for g in range(8):
        gcol[g * 16 : (g + 1) * 16] = guide[PLACE[g] * 16 : (PLACE[g] + 1) * 16]

    mark("p04_sumwait")
    arrived(recv_b, recv_of["b"])
    qkv = recv_b[0].astype(F32)
    for i in range(1, DP):
        qkv = qkv + recv_b[i].astype(F32)

    mark("p05_rope")

    def turn(v):
        return v * cosine + pltpu.roll(v, 64, 1) * sine

    for g in range(8):
        q_s[:, g, :] = turn(qkv[:, g * HEAD : (g + 1) * HEAD])
    k_new = turn(qkv[:, 1024:1152]).astype(BF16).astype(F32)
    v_new = qkv[:, 1152:1280].astype(BF16).astype(F32)

    mark("p06_attn")
    l_k.wait()
    l_v.wait()
    scale = HEAD ** (-0.5)
    slot_at = lax.broadcasted_iota(jnp.int32, (8, 256), 1)
    for start in (0, 8):
        prompts = range(start, start + 8)
        q = [q_s[p].astype(BF16) for p in prompts]
        scores = [
            lax.dot_general(
                q[p - start], k_v[p], (((1,), (1,)), ((), ())), preferred_element_type=F32
            )
            for p in prompts
        ]
        k_own = jnp.concatenate([jnp.broadcast_to(k_new[p : p + 1], (8, HEAD)) for p in prompts])
        v_own = jnp.concatenate([jnp.broadcast_to(v_new[p : p + 1], (8, HEAD)) for p in prompts])
        q_all = jnp.concatenate([v.astype(F32) for v in q])
        e_own = jnp.exp(jnp.sum(q_all * k_own, axis=1, keepdims=True) * scale)
        e = jnp.concatenate(
            [
                jnp.where(slot_at < lens[0, p], jnp.exp(scores[p - start] * scale), 0.0)
                for p in prompts
            ]
        )
        den = jnp.sum(e, axis=1, keepdims=True) + e_own
        w = (e / den).astype(BF16)
        w_own = (e_own / den).astype(BF16).astype(F32)
        o = jnp.concatenate(
            [
                jnp.dot(
                    w[(p - start) * 8 : (p - start + 1) * 8],
                    v_v[p],
                    preferred_element_type=F32,
                )
                for p in prompts
            ]
        )
        att_s[pl.ds(start, 8)] = (o + w_own * v_own).reshape(8, 8, HEAD)
    for g in range(8):
        att_b[:, pl.ds(g * HEAD, HEAD)] = att_s[:, g, :].astype(BF16)

    mark("p07_gatherC")
    core = D % 2
    slot = c * 8 + D // 2
    for dx, dy in PLANE:
        if (dx, dy) != (0, 0):
            to = peer(dx, dy)
            remote(att_b, att_all.at[slot], send_of["c"], c_recv.at[x], (S, to, zl * 2 + core))

    @pl.when(core == c)
    def _():
        pltpu.make_async_copy(att_b, att_all.at[slot], c_recv.at[x]).start()

    @pl.when(core != c)
    def _():
        remote(att_b, att_all.at[slot], send_of["c"], c_recv.at[x], sib)

    l_wo.wait()
    arrived(wo_v.at[1 - c], w_recv.at[2])

    for pair in ((2, 1), (3, 0)):
        blocks = [(x + dx) % RING for dx in pair]
        for block in blocks:
            arrived(att_all.at[pl.ds(0, 4)], c_recv.at[block])
        mark(f"p08_outproj{pair[0]}")
        a0 = jnp.concatenate([att_all[pl.ds(2 * b, 2)].reshape(32, 1024) for b in blocks])
        a1 = jnp.concatenate([att_all[pl.ds(8 + 2 * b, 2)].reshape(32, 1024) for b in blocks])
        for n in range(2):
            cols = pl.ds(n * 256, 256)
            r = jnp.dot(a0, wo_v[0, :, cols], preferred_element_type=F32)
            r = r + jnp.dot(a1, wo_v[1, :, cols], preferred_element_type=F32)
            for m, block in enumerate(blocks):
                part_d[block, :, cols] = r[m * 32 : (m + 1) * 32].astype(BF16)
        for block in blocks:
            other = (block // 2 - S) * (block // 2 - S)
            to = (1 - other) * (1 + block % 2) + other * 3 * (block % 2)

            @pl.when(to != zl)
            def _():
                remote(
                    part_d.at[block],
                    recv_d.at[(zl - to + 3) % 4],
                    send_of["d"],
                    recv_of["d"],
                    (S, D, to * 2 + c),
                )
        mark(f"p08b_wait{pair[0]}")

    def owned(z):
        inner = ((z + 1) // 2) % 2
        half = inner * S + (1 - inner) * (1 - S)
        return half, 2 * half + inner * (z - 1) + (1 - inner) * (z // 3)

    mark("p09_sumwaitD")
    my_half, mine = owned(zl)
    my_j = 2 * (mine % 2) + c
    total = h_c[pl.ds(2 * mine, 2)].reshape(32, 512).astype(F32) + part_d[mine].astype(F32)
    arrived(recv_d, recv_of["d"])
    for i in range(3):
        total = total + recv_d[i].astype(F32)
    resid[...] = total.astype(BF16)

    mark("p10_z")
    place = buf.at[S, D, pl.ds(my_j * 32, 32), :]
    for z in range(4):
        at_home = jnp.logical_and(my_half == S, 2 * z + S == T)

        @pl.when(at_home)
        def _():
            pltpu.make_async_copy(resid, place, z_recv.at[my_j]).start()

        @pl.when(jnp.logical_not(at_home))
        def _():
            remote(resid, place, send_of["z"], z_recv.at[my_j], (my_half, D, 2 * z + S))

    arrived(gain_all.at[pl.ds(0, DP - 1)], recv_of["gain"])
    l_wh.wait()
    acc[...] = jnp.zeros_like(acc)
    ssq[...] = jnp.zeros_like(ssq)

    def neighbour(name, step):
        if name == "x":
            return (S, ((x + RING + step) % RING) * RING + y, T)
        return (S, x * RING + (y + RING + step) % RING, T)

    def slot_of(dx, dy):
        return ((x + RING - dx) % RING) * RING + (y + RING - dy) % RING

    def send_on(piece, hops):
        slot, quarter = slot_of(*piece[:2]), piece[2]
        rows = buf.at[c, slot, pl.ds(quarter * 32, 32), :]
        for hop in hops:
            remote(rows, rows, send_of["f"], f_recv.at[slot, quarter], neighbour(*hop))

    def share(dx, dy):
        whole = buf.at[c, slot_of(dx, dy)]
        remote(whole, whole, send_of["sib"], sib_recv.at[slot_of(dx, dy)], sib)

    def head(dx, dy):
        slot = slot_of(dx, dy)
        arrived(buf.at[1 - c, slot], sib_recv.at[slot])
        v = buf[:, slot].reshape(256, 512).astype(F32)
        v2 = v * v
        ssq[...] += v2[:, 0:128] + v2[:, 128:256] + v2[:, 256:384] + v2[:, 384:512]
        w = (v * gain_all[slot]).astype(BF16)
        acc[...] += jnp.dot(
            w,
            wh_v[pl.ds(pl.multiple_of(slot * 512, 512), 512), :],
            preferred_element_type=F32,
        )

    mark("p10b_zwait")
    for quarter in range(4):
        arrived(buf.at[c, D, pl.ds(quarter * 32, 32), :], z_recv.at[quarter])
        send_on((0, 0, quarter), HOPS[(0, 0, quarter)][:2])
    mark("p11_own")
    for quarter in range(4):
        send_on((0, 0, quarter), HOPS[(0, 0, quarter)][2:])
    share(0, 0)
    complete = [(0, (0, 0))]
    held = {}
    for n, piece in enumerate(ORDER):
        if n % 10 == 0:
            mark(f"p12_pieces{n:02d}")
        dx, dy, quarter = piece
        slot = slot_of(dx, dy)
        arrived(buf.at[c, slot, pl.ds(quarter * 32, 32), :], f_recv.at[slot, quarter])
        send_on(piece, forwards(piece))
        held[dx, dy] = held.get((dx, dy), 0) + 1
        if held[dx, dy] == 4:
            share(dx, dy)
            complete.append((n, (dx, dy)))
        if complete and n - complete[0][0] >= 8:
            head(*complete.pop(0)[1])
    mark("p13_lastheads")
    for _, offset in complete:
        head(*offset)

    mark("p16_guided")
    inv = lax.rsqrt(jnp.sum(ssq[...], axis=1, keepdims=True) / WIDTH + norm_eps)
    cond = acc[0:128, :] * inv[0:128]
    uncond = acc[128:256, :] * inv[128:256]
    guide = gcol[:, 0:1]
    guided = uncond + guide * (cond - uncond) - counts[...]
    acc[0:128, :] = guided
    e = jnp.exp(guided)
    e = e[:, 0:128] + e[:, 128:256] + e[:, 256:384] + e[:, 384:512]
    mark("p17_total")
    tot_one[...] = jnp.sum(jnp.transpose(e), axis=0, keepdims=True)

    for n, (dx, dy) in enumerate(PLANE):
        for dt in range(TEN):
            if (dx, dy, dt) != (0, 0, 0):
                to = (S, peer(dx, dy), (T + dt) % TEN)
                remote(tot_one, tot_all.at[n * TEN + dt - n // 15], send_of["t"], recv_of["t"], to)
    arrived(tot_all, recv_of["t"])
    mark("p18_out")
    totals = tot_one[...] + jnp.sum(tot_all[...], axis=0)
    log_total = jnp.transpose(jnp.broadcast_to(jnp.log(totals), (128, 128)))
    for g in range(8):
        for n in range(4):
            cols = pl.ds(n * 128, 128)
            out[pl.ds(PLACE[g] * 16, 16), cols] = (
                acc[pl.ds(g * 16, 16), cols] - log_total[g * 16 : (g + 1) * 16]
            )

    mark("p19_waitsend")
    left(wq_v.at[0], "w")
    left(kv_v.at[0], "w")
    left(wo_v.at[0], "w")
    left(h_c.at[pl.ds(0, 7)], "a")
    left(gain_all.at[pl.ds(0, DP - 1)], "gain")
    left(part_d.at[pl.ds(0, 3)], "d")
    left(buf.at[0, pl.ds(0, 15)], "f")
    left(buf.at[0], "sib")
    left(tot_all, "t")
    kept_c = core == c
    kept_z = jnp.logical_and(my_half == S, c == S)

    @pl.when(kept_c)
    def _():
        left(recv_b.at[pl.ds(0, DP - 1)], "b")
        left(att_all.at[pl.ds(0, DP - 1)], "c")

    @pl.when(jnp.logical_not(kept_c))
    def _():
        left(recv_b, "b")
        left(att_all, "c")

    @pl.when(kept_z)
    def _():
        left(part_d.at[pl.ds(0, 3)], "z")

    @pl.when(jnp.logical_not(kept_z))
    def _():
        left(part_d, "z")

    mark(None)


def body(hidden, keys, vals, lens, ids, guid, wq, kvw, wo, gain, wh):
    dma = pltpu.SemaphoreType.DMA
    anywhere = pl.BlockSpec(memory_space=pl.ANY)
    vmem = pl.BlockSpec(memory_space=pltpu.VMEM)
    smem = pl.BlockSpec(memory_space=pltpu.SMEM)
    return pl.pallas_call(
        kernel,
        out_shape=jax.ShapeDtypeStruct((128, 512), F32),
        in_specs=[
            anywhere,
            anywhere,
            anywhere,
            smem,
            anywhere,
            vmem,
            anywhere,
            anywhere,
            anywhere,
            vmem,
            anywhere,
        ],
        out_specs=vmem,
        scratch_shapes=[
            pltpu.VMEM((TEN, 16, 512), BF16),
            pltpu.VMEM((2, 512, 1024), BF16),
            pltpu.VMEM((512, 2, 128), BF16),
            pltpu.VMEM((2, 512, 256), BF16),
            pltpu.VMEM((16, 256, 128), BF16),
            pltpu.VMEM((16, 256, 128), BF16),
            pltpu.VMEM((2, 1024, 512), BF16),
            pltpu.VMEM((8192, 512), BF16),
            pltpu.VMEM((128, 128), jnp.int32),
            pltpu.VMEM((DP, 1, 512), F32),
            pltpu.VMEM((8, 2, 16, 1280), BF16),
            pltpu.VMEM((DP, 16, 1280), BF16),
            pltpu.VMEM((16, 8, 128), F32),
            pltpu.VMEM((16, 8, 128), F32),
            pltpu.VMEM((16, 1024), BF16),
            pltpu.VMEM((DP, 16, 1024), BF16),
            pltpu.VMEM((4, 32, 512), BF16),
            pltpu.VMEM((3, 32, 512), BF16),
            pltpu.VMEM((32, 512), BF16),
            pltpu.VMEM((2, DP, 128, 512), BF16),
            pltpu.VMEM((256, 512), F32),
            pltpu.VMEM((256, 128), F32),
            pltpu.VMEM((128, 512), F32),
            pltpu.VMEM((128, 128), F32),
            pltpu.VMEM((1, 128), F32),
            pltpu.VMEM((DP * TEN - 1, 1, 128), F32),
            dma((9,)),
            dma((3,)),
            dma((4,)),
            dma((4,)),
            dma((DP, 4)),
            dma((DP,)),
            dma((20,)),
        ],
        compiler_params=pltpu.CompilerParams(
            collective_id=0, has_side_effects=True, vmem_limit_bytes=60 * 1024 * 1024
        ),
    )(hidden, keys, vals, lens, ids, guid.reshape(2, 128), wq, kvw, wo, gain, wh)


def solution(mesh):
    return jax.shard_map(
        body,
        mesh=mesh,
        in_specs=(
            P("stream", "tensor", "dp"),
            P("stream", "dp", "tensor", None, None),
            P("stream", "dp", "tensor", None, None),
            P("stream", "dp"),
            P(),
            P(),
            P("dp", "tensor"),
            P("dp", None, "tensor"),
            P("tensor", "dp"),
            P("dp"),
            P(None, ("dp", "tensor")),
        ),
        out_specs=P("stream", ("dp", "tensor")),
        check_vma=False,
    )
```

```python
import heapq

import jax
import jax.numpy as jnp
from jax import lax
from jax.experimental import pallas as pl
from jax.experimental.pallas import tpu as pltpu
from jax.sharding import PartitionSpec as P

MESH = pl.DeviceIdType.MESH
F32 = jnp.float32
BF16 = jnp.bfloat16
WIDTH = 8192
HEAD = 128
RING = 4
DP = 16
TEN = 8

rope_theta = 500000.0
penalty_step = 1.5
norm_eps = 1e-05


MARKS = False
open_scope = []


def mark(name):
    if MARKS:
        if open_scope:
            open_scope.pop().__exit__(None, None, None)
        if name:
            open_scope.append(jax.named_scope(name))
            open_scope[0].__enter__()


def routes():
    found = []
    for depth in range(5):
        for dx in range(RING):
            for dy in range(RING):
                if min(dx, RING - dx) + min(dy, RING - dy) != depth:
                    continue
                for quarter in range(4):
                    first, second = (dx, dy) if quarter < 2 else (dy, dx)
                    names = ("x", "y") if quarter < 2 else ("y", "x")
                    odd = quarter % 2
                    hops = []
                    if second == 0:
                        if first == 0:
                            hops += [(names[0], 1), (names[0], -1)]
                        elif first == 1 and not odd:
                            hops += [(names[0], 1)]
                        elif first == 3 and odd:
                            hops += [(names[0], -1)]
                        hops += [(names[1], 1), (names[1], -1)]
                    elif second == 1 and not odd:
                        hops += [(names[1], 1)]
                    elif second == 3 and odd:
                        hops += [(names[1], -1)]
                    found.append((depth, dx, dy, quarter, hops))
    return found


HOPS = {r[1:4]: r[4] for r in routes()}
N_FORWARD = sum(len(hops) for hops in HOPS.values())
PLACE = [4 * (g // 4) + 2 * (g % 2) + (g // 2) % 2 for g in range(8)]


def onward(piece, hop):
    dx, dy, quarter = piece
    axis, step = hop
    if axis == "x":
        return (dx + step) % RING, dy, quarter
    return dx, (dy + step) % RING, quarter


def further(piece):
    return max([1 + further(onward(piece, hop)) for hop in HOPS[piece]], default=0)


def forwards(piece):
    return sorted(HOPS[piece], key=lambda hop: -further(onward(piece, hop)))


def plan():
    free, arrivals, order = {}, [], []

    def send(piece, hop, now):
        free[hop] = max(free.get(hop, 0.0), now) + 0.7
        heapq.heappush(arrivals, (free[hop] + 1.66, len(order), onward(piece, hop)))

    own = [(0, 0, quarter) for quarter in range(4)]
    first = [(piece, hop) for piece in own for hop in HOPS[piece][:2]]
    first += [(piece, hop) for piece in own for hop in HOPS[piece][2:]]
    for piece, hop in first:
        send(piece, hop, 0.0)
    now = 0.0
    while arrivals:
        when, _, piece = heapq.heappop(arrivals)
        now = max(now, when) + 0.02
        order.append(piece)
        for hop in forwards(piece):
            send(piece, hop, now)
    return order


ORDER = plan()
FAR = (2, 1, 3, 0)
PLANE = sorted(
    [(dx, dy) for dx in range(RING) for dy in range(RING)],
    key=lambda o: -min(o[0], RING - o[0]) - min(o[1], RING - o[1]),
)


def kernel(
    hidden,
    keys,
    vals,
    lens,
    ids,
    guid,
    wq,
    kvw,
    wo,
    gain,
    wh,
    out,
    h_c,
    wq_v,
    kvw_v,
    kv_v,
    k_v,
    v_v,
    wo_v,
    wh_v,
    ids_v,
    gain_all,
    part,
    recv_b,
    q_s,
    att_s,
    att_b,
    att_all,
    part_d,
    recv_d,
    resid,
    buf,
    acc,
    ssq,
    counts,
    gcol,
    tot_one,
    tot_all,
    gain_v,
    lens_v,
    guid_v,
    load_sem,
    w_recv,
    z_recv,
    c_recv,
    f_recv,
    sib_recv,
    one,
):
    S = lax.axis_index("stream")
    D = lax.axis_index("dp")
    T = lax.axis_index("tensor")
    zl, c = T // 2, T % 2
    x, y = D // RING, D % RING
    sib = (S, D, zl * 2 + 1 - c)
    names = ("w", "a", "gain", "b", "c", "d", "z", "f", "sib", "t")
    send_of = {name: one.at[n] for n, name in enumerate(names)}
    recv_of = {name: one.at[len(names) + n] for n, name in enumerate(names)}

    def remote(src, dst, ssem, rsem, dev):
        copy = pltpu.make_async_remote_copy(
            src_ref=src,
            dst_ref=dst,
            send_sem=ssem,
            recv_sem=rsem,
            device_id=dev,
            device_id_type=MESH,
        )
        copy.start()

    def arrived(ref, rsem):
        pltpu.make_async_remote_copy(
            src_ref=ref,
            dst_ref=ref,
            send_sem=send_of["w"],
            recv_sem=rsem,
            device_id=sib,
            device_id_type=MESH,
        ).wait_recv()

    def left(ref, name):
        pltpu.make_async_remote_copy(
            src_ref=ref,
            dst_ref=ref,
            send_sem=send_of[name],
            recv_sem=recv_of[name],
            device_id=sib,
            device_id_type=MESH,
        ).wait_send()

    def peer(dx, dy):
        return ((x + dx) % RING) * RING + (y + dy) % RING

    mark("p00_entry")
    barrier = pltpu.get_barrier_semaphore()
    for i in range(1, DP):
        pl.semaphore_signal(
            barrier, inc=1, device_id=(S, (D + i) % DP, T), device_id_type=MESH
        )
        pl.semaphore_signal(
            barrier, inc=1, device_id=(S, (D + i) % DP, zl * 2 + 1 - c), device_id_type=MESH
        )
    for i in range(1, 16):
        other = (S * TEN + T + i) % 16
        pl.semaphore_signal(
            barrier, inc=1, device_id=(other // TEN, D, other % TEN), device_id_type=MESH
        )

    loads = []

    def load(src, dst, sem=None):
        if sem is None:
            sem = load_sem.at[len(loads)]
            loads.append(sem)
        copy = pltpu.make_async_copy(src, dst, sem)
        copy.start()
        return copy

    load(hidden.at[0, pl.ds(c * 16, 16)], h_c.at[T], recv_of["a"])
    l_gain = load(gain, gain_v)
    l_lens = load(lens, lens_v)
    l_guid = load(guid, guid_v)
    l_wq = load(wq, wq_v.at[c])
    l_kv = load(kvw, kvw_v)
    for g in range(8):
        load(
            ids.at[pl.ds(S * 128 + PLACE[g] * 16, 16), :],
            ids_v.at[pl.ds(g * 16, 16), :],
            load_sem.at[11],
        )
    l_k = load(keys.at[0, :, 0], k_v)
    l_v = load(vals.at[0, :, 0], v_v)
    l_wo = load(wo, wo_v.at[c])
    pl.semaphore_wait(barrier, 45)

    mark("p01_hidden")
    for dz in (3, 2, 1):
        for core in (0, 1):
            dev = (S, D, ((zl + dz) % 4) * 2 + core)
            remote(
                hidden.at[0, pl.ds(core * 16, 16)], h_c.at[T], send_of["a"], recv_of["a"], dev
            )
    remote(hidden.at[0, pl.ds(16 - c * 16, 16)], h_c.at[T], send_of["a"], recv_of["a"], sib)
    remote(wq, wq_v.at[c], send_of["w"], w_recv.at[0], sib)
    l_gain.wait()
    gain_all[D] = gain_v[...].astype(F32).reshape(1, 512)
    l_wh = load(wh, wh_v)
    remote(wo, wo_v.at[c], send_of["w"], w_recv.at[2], sib)
    l_kv.wait()
    for n in range(2):
        kv_v[c, :, n * 128 : (n + 1) * 128] = kvw_v[:, n, :]
    l_wq.wait()
    remote(kv_v.at[c], kv_v.at[c], send_of["w"], w_recv.at[1], sib)
    arrived(h_c, recv_of["a"])

    mark("p02_qkv")
    h = h_c[...].reshape(128, 512)
    for i in range(2):
        g = (c + i) % 2
        if i == 1:
            arrived(wq_v.at[g], w_recv.at[0])
            arrived(kv_v.at[g], w_recv.at[1])
        for n in range(4):
            cols = pl.ds(n * 256, 256)
            r = jnp.dot(h, wq_v[g, :, cols], preferred_element_type=F32)
            part[:, g, :, cols] = r.reshape(8, 16, 256).astype(BF16)
        r = jnp.dot(h, kv_v[g], preferred_element_type=F32)
        part[:, g, :, pl.ds(1024, 256)] = r.reshape(8, 16, 256).astype(BF16)
        for n in range(8):
            to = peer(FAR[n // 2], (y + c) % 2 + 2 - 2 * (n % 2))
            k = to // 2
            if i == 1:
                remote(
                    part.at[k, g], recv_b.at[D], send_of["b"], recv_of["b"], (S, to, zl * 2 + g)
                )
                continue

            @pl.when(to == D)
            def _():
                pltpu.make_async_copy(part.at[k, g], recv_b.at[D], recv_of["b"]).start()

            @pl.when(to != D)
            def _():
                remote(
                    part.at[k, g], recv_b.at[D], send_of["b"], recv_of["b"], (S, to, zl * 2 + g)
                )
    for i in range(1, DP):
        to = (D + i) % DP
        remote(gain_all.at[D], gain_all.at[D], send_of["gain"], recv_of["gain"], (S, to, T))

    mark("p03_tables")
    lane = lax.broadcasted_iota(jnp.int32, (16, HEAD), 1)
    row = lax.broadcasted_iota(jnp.int32, (16, HEAD), 0)
    freq = jnp.exp(((lane % 64).astype(F32) * (2.0 / HEAD)) * (-jnp.log(F32(rope_theta))))
    l_lens.wait()
    l_guid.wait()
    position = jnp.zeros((16, HEAD), jnp.int32)
    for p in range(16):
        position = jnp.where(row == p, lens_v[0, p], position)
    angle = position.astype(F32) * freq
    cosine = jnp.cos(angle)
    sine = jnp.sin(angle) * jnp.where(lane < 64, -1.0, 1.0)

    pltpu.make_async_copy(ids.at[pl.ds(0, 128), :], ids_v, load_sem.at[11]).wait()
    base = (D * TEN + T) * 512
    ids_v[...] = jnp.transpose(ids_v[...]) - base
    for n in range(4):
        column = lax.broadcasted_iota(jnp.int32, (128, 128), 0) + n * 128

        def add(r, total):
            for k in range(8):
                here = ids_v[pl.ds(r * 8 + k, 1), :]
                total = total + jnp.where(column == here, 1.0, 0.0)
            return total

        total = lax.fori_loop(0, 16, add, jnp.zeros((128, 128), F32))
        counts[:, pl.ds(n * 128, 128)] = jnp.transpose(total) * penalty_step
    guide = jnp.transpose(jnp.broadcast_to(guid_v[pl.ds(S, 1), :], (128, 128)))
    for g in range(8):
        gcol[g * 16 : (g + 1) * 16] = guide[PLACE[g] * 16 : (PLACE[g] + 1) * 16]

    mark("p04_sumwait")
    arrived(recv_b, recv_of["b"])
    qkv = recv_b[0].astype(F32)
    for i in range(1, DP):
        qkv = qkv + recv_b[i].astype(F32)

    mark("p05_rope")

    def turn(v):
        return v * cosine + pltpu.roll(v, 64, 1) * sine

    for g in range(8):
        q_s[:, g, :] = turn(qkv[:, g * HEAD : (g + 1) * HEAD])
    k_new = turn(qkv[:, 1024:1152]).astype(BF16).astype(F32)
    v_new = qkv[:, 1152:1280].astype(BF16).astype(F32)

    mark("p06_attn")
    l_k.wait()
    l_v.wait()
    scale = HEAD ** (-0.5)
    slot_at = lax.broadcasted_iota(jnp.int32, (8, 256), 1)
    for start in (0, 8):
        prompts = range(start, start + 8)
        q = [q_s[p].astype(BF16) for p in prompts]
        scores = [
            lax.dot_general(
                q[p - start], k_v[p], (((1,), (1,)), ((), ())), preferred_element_type=F32
            )
            for p in prompts
        ]
        k_own = jnp.concatenate([jnp.broadcast_to(k_new[p : p + 1], (8, HEAD)) for p in prompts])
        v_own = jnp.concatenate([jnp.broadcast_to(v_new[p : p + 1], (8, HEAD)) for p in prompts])
        q_all = jnp.concatenate([v.astype(F32) for v in q])
        e_own = jnp.exp(jnp.sum(q_all * k_own, axis=1, keepdims=True) * scale)
        e = jnp.concatenate(
            [
                jnp.where(slot_at < lens_v[0, p], jnp.exp(scores[p - start] * scale), 0.0)
                for p in prompts
            ]
        )
        den = jnp.sum(e, axis=1, keepdims=True) + e_own
        w = (e / den).astype(BF16)
        w_own = (e_own / den).astype(BF16).astype(F32)
        o = jnp.concatenate(
            [
                jnp.dot(
                    w[(p - start) * 8 : (p - start + 1) * 8],
                    v_v[p],
                    preferred_element_type=F32,
                )
                for p in prompts
            ]
        )
        att_s[pl.ds(start, 8)] = (o + w_own * v_own).reshape(8, 8, HEAD)
    for g in range(8):
        att_b[:, pl.ds(g * HEAD, HEAD)] = att_s[:, g, :].astype(BF16)

    mark("p07_gatherC")
    core = D % 2
    slot = c * 8 + D // 2
    for dx, dy in PLANE:
        if (dx, dy) != (0, 0):
            to = peer(dx, dy)
            remote(att_b, att_all.at[slot], send_of["c"], c_recv.at[x], (S, to, zl * 2 + core))

    @pl.when(core == c)
    def _():
        pltpu.make_async_copy(att_b, att_all.at[slot], c_recv.at[x]).start()

    @pl.when(core != c)
    def _():
        remote(att_b, att_all.at[slot], send_of["c"], c_recv.at[x], sib)

    l_wo.wait()
    arrived(wo_v.at[1 - c], w_recv.at[2])

    for pair in ((2, 1), (3, 0)):
        blocks = [(x + dx) % RING for dx in pair]
        for block in blocks:
            arrived(att_all.at[pl.ds(0, 4)], c_recv.at[block])
        mark(f"p08_outproj{pair[0]}")
        a0 = jnp.concatenate([att_all[pl.ds(2 * b, 2)].reshape(32, 1024) for b in blocks])
        a1 = jnp.concatenate([att_all[pl.ds(8 + 2 * b, 2)].reshape(32, 1024) for b in blocks])
        for n in range(2):
            cols = pl.ds(n * 256, 256)
            r = jnp.dot(a0, wo_v[0, :, cols], preferred_element_type=F32)
            r = r + jnp.dot(a1, wo_v[1, :, cols], preferred_element_type=F32)
            for m, block in enumerate(blocks):
                part_d[block, :, cols] = r[m * 32 : (m + 1) * 32].astype(BF16)
        for block in blocks:
            other = (block // 2 - S) * (block // 2 - S)
            to = (1 - other) * (1 + block % 2) + other * 3 * (block % 2)

            @pl.when(to != zl)
            def _():
                remote(
                    part_d.at[block],
                    recv_d.at[(zl - to + 3) % 4],
                    send_of["d"],
                    recv_of["d"],
                    (S, D, to * 2 + c),
                )
        mark(f"p08b_wait{pair[0]}")

    def owned(z):
        inner = ((z + 1) // 2) % 2
        half = inner * S + (1 - inner) * (1 - S)
        return half, 2 * half + inner * (z - 1) + (1 - inner) * (z // 3)

    mark("p09_sumwaitD")
    my_half, mine = owned(zl)
    my_j = 2 * (mine % 2) + c
    total = h_c[pl.ds(2 * mine, 2)].reshape(32, 512).astype(F32) + part_d[mine].astype(F32)
    arrived(recv_d, recv_of["d"])
    for i in range(3):
        total = total + recv_d[i].astype(F32)
    resid[...] = total.astype(BF16)

    mark("p10_z")
    place = buf.at[S, D, pl.ds(my_j * 32, 32), :]
    for z in range(4):
        at_home = jnp.logical_and(my_half == S, 2 * z + S == T)

        @pl.when(at_home)
        def _():
            pltpu.make_async_copy(resid, place, z_recv.at[my_j]).start()

        @pl.when(jnp.logical_not(at_home))
        def _():
            remote(resid, place, send_of["z"], z_recv.at[my_j], (my_half, D, 2 * z + S))

    arrived(gain_all.at[pl.ds(0, DP - 1)], recv_of["gain"])
    l_wh.wait()
    acc[...] = jnp.zeros_like(acc)
    ssq[...] = jnp.zeros_like(ssq)

    def neighbour(name, step):
        if name == "x":
            return (S, ((x + RING + step) % RING) * RING + y, T)
        return (S, x * RING + (y + RING + step) % RING, T)

    def slot_of(dx, dy):
        return ((x + RING - dx) % RING) * RING + (y + RING - dy) % RING

    def send_on(piece, hops):
        slot, quarter = slot_of(*piece[:2]), piece[2]
        rows = buf.at[c, slot, pl.ds(quarter * 32, 32), :]
        for hop in hops:
            remote(rows, rows, send_of["f"], f_recv.at[slot, quarter], neighbour(*hop))

    def share(dx, dy):
        whole = buf.at[c, slot_of(dx, dy)]
        remote(whole, whole, send_of["sib"], sib_recv.at[slot_of(dx, dy)], sib)

    def head(dx, dy):
        slot = slot_of(dx, dy)
        arrived(buf.at[1 - c, slot], sib_recv.at[slot])
        v = buf[:, slot].reshape(256, 512).astype(F32)
        v2 = v * v
        ssq[...] += v2[:, 0:128] + v2[:, 128:256] + v2[:, 256:384] + v2[:, 384:512]
        w = (v * gain_all[slot]).astype(BF16)
        acc[...] += jnp.dot(
            w,
            wh_v[pl.ds(pl.multiple_of(slot * 512, 512), 512), :],
            preferred_element_type=F32,
        )

    mark("p10b_zwait")
    for quarter in range(4):
        arrived(buf.at[c, D, pl.ds(quarter * 32, 32), :], z_recv.at[quarter])
        send_on((0, 0, quarter), HOPS[(0, 0, quarter)][:2])
    mark("p11_own")
    for quarter in range(4):
        send_on((0, 0, quarter), HOPS[(0, 0, quarter)][2:])
    share(0, 0)
    complete = [(0, (0, 0))]
    held = {}
    for n, piece in enumerate(ORDER):
        if n % 10 == 0:
            mark(f"p12_pieces{n:02d}")
        dx, dy, quarter = piece
        slot = slot_of(dx, dy)
        arrived(buf.at[c, slot, pl.ds(quarter * 32, 32), :], f_recv.at[slot, quarter])
        send_on(piece, forwards(piece))
        held[dx, dy] = held.get((dx, dy), 0) + 1
        if held[dx, dy] == 4:
            share(dx, dy)
            complete.append((n, (dx, dy)))
        if complete and n - complete[0][0] >= 8:
            head(*complete.pop(0)[1])
    mark("p13_lastheads")
    for _, offset in complete:
        head(*offset)

    mark("p16_guided")
    inv = lax.rsqrt(jnp.sum(ssq[...], axis=1, keepdims=True) / WIDTH + norm_eps)
    cond = acc[0:128, :] * inv[0:128]
    uncond = acc[128:256, :] * inv[128:256]
    guide = gcol[:, 0:1]
    guided = uncond + guide * (cond - uncond) - counts[...]
    acc[0:128, :] = guided
    e = jnp.exp(guided)
    e = e[:, 0:128] + e[:, 128:256] + e[:, 256:384] + e[:, 384:512]
    mark("p17_total")
    tot_one[...] = jnp.sum(jnp.transpose(e), axis=0, keepdims=True)

    for n, (dx, dy) in enumerate(PLANE):
        for dt in range(TEN):
            if (dx, dy, dt) != (0, 0, 0):
                to = (S, peer(dx, dy), (T + dt) % TEN)
                remote(tot_one, tot_all.at[n * TEN + dt - n // 15], send_of["t"], recv_of["t"], to)
    arrived(tot_all, recv_of["t"])
    mark("p18_out")
    totals = tot_one[...] + jnp.sum(tot_all[...], axis=0)
    log_total = jnp.transpose(jnp.broadcast_to(jnp.log(totals), (128, 128)))
    for g in range(8):
        for n in range(4):
            cols = pl.ds(n * 128, 128)
            out[pl.ds(PLACE[g] * 16, 16), cols] = (
                acc[pl.ds(g * 16, 16), cols] - log_total[g * 16 : (g + 1) * 16]
            )

    mark("p19_waitsend")
    left(wq_v.at[0], "w")
    left(kv_v.at[0], "w")
    left(wo_v.at[0], "w")
    left(h_c.at[pl.ds(0, 7)], "a")
    left(gain_all.at[pl.ds(0, DP - 1)], "gain")
    left(part_d.at[pl.ds(0, 3)], "d")
    left(buf.at[0, pl.ds(0, 15)], "f")
    left(buf.at[0], "sib")
    left(tot_all, "t")
    kept_c = core == c
    kept_z = jnp.logical_and(my_half == S, c == S)

    @pl.when(kept_c)
    def _():
        left(recv_b.at[pl.ds(0, DP - 1)], "b")
        left(att_all.at[pl.ds(0, DP - 1)], "c")

    @pl.when(jnp.logical_not(kept_c))
    def _():
        left(recv_b, "b")
        left(att_all, "c")

    @pl.when(kept_z)
    def _():
        left(part_d.at[pl.ds(0, 3)], "z")

    @pl.when(jnp.logical_not(kept_z))
    def _():
        left(part_d, "z")

    mark(None)


def body(hidden, keys, vals, lens, ids, guid, wq, kvw, wo, gain, wh):
    dma = pltpu.SemaphoreType.DMA
    anywhere = pl.BlockSpec(memory_space=pl.ANY)
    vmem = pl.BlockSpec(memory_space=pltpu.VMEM)
    return pl.pallas_call(
        kernel,
        out_shape=pltpu.VMEM((128, 512), F32),
        in_specs=[anywhere] * 11,
        out_specs=vmem,
        scratch_shapes=[
            pltpu.VMEM((TEN, 16, 512), BF16),
            pltpu.VMEM((2, 512, 1024), BF16),
            pltpu.VMEM((512, 2, 128), BF16),
            pltpu.VMEM((2, 512, 256), BF16),
            pltpu.VMEM((16, 256, 128), BF16),
            pltpu.VMEM((16, 256, 128), BF16),
            pltpu.VMEM((2, 1024, 512), BF16),
            pltpu.VMEM((8192, 512), BF16),
            pltpu.VMEM((128, 128), jnp.int32),
            pltpu.VMEM((DP, 1, 512), F32),
            pltpu.VMEM((8, 2, 16, 1280), BF16),
            pltpu.VMEM((DP, 16, 1280), BF16),
            pltpu.VMEM((16, 8, 128), F32),
            pltpu.VMEM((16, 8, 128), F32),
            pltpu.VMEM((16, 1024), BF16),
            pltpu.VMEM((DP, 16, 1024), BF16),
            pltpu.VMEM((4, 32, 512), BF16),
            pltpu.VMEM((3, 32, 512), BF16),
            pltpu.VMEM((32, 512), BF16),
            pltpu.VMEM((2, DP, 128, 512), BF16),
            pltpu.VMEM((256, 512), F32),
            pltpu.VMEM((256, 128), F32),
            pltpu.VMEM((128, 512), F32),
            pltpu.VMEM((128, 128), F32),
            pltpu.VMEM((1, 128), F32),
            pltpu.VMEM((DP * TEN - 1, 1, 128), F32),
            pltpu.VMEM((512,), BF16),
            pltpu.SMEM((1, 16), jnp.int32),
            pltpu.VMEM((2, 128), F32),
            dma((12,)),
            dma((3,)),
            dma((4,)),
            dma((4,)),
            dma((DP, 4)),
            dma((DP,)),
            dma((20,)),
        ],
        compiler_params=pltpu.CompilerParams(
            collective_id=0, has_side_effects=True, vmem_limit_bytes=60 * 1024 * 1024
        ),
    )(hidden, keys, vals, lens, ids, guid.reshape(2, 128), wq, kvw, wo, gain, wh)


def solution(mesh):
    return jax.shard_map(
        body,
        mesh=mesh,
        in_specs=(
            P("stream", "tensor", "dp"),
            P("stream", "dp", "tensor", None, None),
            P("stream", "dp", "tensor", None, None),
            P("stream", "dp"),
            P(),
            P(),
            P("dp", "tensor"),
            P("dp", None, "tensor"),
            P("tensor", "dp"),
            P("dp"),
            P(None, ("dp", "tensor")),
        ),
        out_specs=P("stream", ("dp", "tensor")),
        check_vma=False,
    )
```

```python
import heapq

import jax
import jax.numpy as jnp
from jax import lax
from jax.experimental import pallas as pl
from jax.experimental.pallas import tpu as pltpu
from jax.sharding import PartitionSpec as P

MESH = pl.DeviceIdType.MESH
F32 = jnp.float32
BF16 = jnp.bfloat16
WIDTH = 8192
HEAD = 128
RING = 4
DP = 16
TEN = 8

rope_theta = 500000.0
penalty_step = 1.5
norm_eps = 1e-05


MARKS = False
open_scope = []


def mark(name):
    if MARKS:
        if open_scope:
            open_scope.pop().__exit__(None, None, None)
        if name:
            open_scope.append(jax.named_scope(name))
            open_scope[0].__enter__()


def routes():
    found = []
    for depth in range(5):
        for dx in range(RING):
            for dy in range(RING):
                if min(dx, RING - dx) + min(dy, RING - dy) != depth:
                    continue
                for quarter in range(4):
                    first, second = (dx, dy) if quarter < 2 else (dy, dx)
                    names = ("x", "y") if quarter < 2 else ("y", "x")
                    odd = quarter % 2
                    hops = []
                    if second == 0:
                        if first == 0:
                            hops += [(names[0], 1), (names[0], -1)]
                        elif first == 1 and not odd:
                            hops += [(names[0], 1)]
                        elif first == 3 and odd:
                            hops += [(names[0], -1)]
                        hops += [(names[1], 1), (names[1], -1)]
                    elif second == 1 and not odd:
                        hops += [(names[1], 1)]
                    elif second == 3 and odd:
                        hops += [(names[1], -1)]
                    found.append((depth, dx, dy, quarter, hops))
    return found


HOPS = {r[1:4]: r[4] for r in routes()}
N_FORWARD = sum(len(hops) for hops in HOPS.values())
PLACE = [4 * (g // 4) + 2 * (g % 2) + (g // 2) % 2 for g in range(8)]


def onward(piece, hop):
    dx, dy, quarter = piece
    axis, step = hop
    if axis == "x":
        return (dx + step) % RING, dy, quarter
    return dx, (dy + step) % RING, quarter


def further(piece):
    return max([1 + further(onward(piece, hop)) for hop in HOPS[piece]], default=0)


def forwards(piece):
    return sorted(HOPS[piece], key=lambda hop: -further(onward(piece, hop)))


def plan():
    free, arrivals, order = {}, [], []

    def send(piece, hop, now):
        free[hop] = max(free.get(hop, 0.0), now) + 0.7
        heapq.heappush(arrivals, (free[hop] + 1.66, len(order), onward(piece, hop)))

    own = [(0, 0, quarter) for quarter in range(4)]
    first = [(piece, hop) for piece in own for hop in HOPS[piece][:2]]
    first += [(piece, hop) for piece in own for hop in HOPS[piece][2:]]
    for piece, hop in first:
        send(piece, hop, 0.0)
    now = 0.0
    while arrivals:
        when, _, piece = heapq.heappop(arrivals)
        now = max(now, when) + 0.02
        order.append(piece)
        for hop in forwards(piece):
            send(piece, hop, now)
    return order


ORDER = plan()


def semaphores():
    number = {}
    keys = [piece if HOPS[piece] else piece[:2] for piece in ORDER]
    for key in keys:
        number.setdefault(key, len(number))
    return {piece: number[key] for piece, key in zip(ORDER, keys)}, len(number)


SEM, N_SEM = semaphores()
LEAVES = {}
for leaf in ORDER:
    if not HOPS[leaf]:
        LEAVES[leaf[:2]] = LEAVES.get(leaf[:2], 0) + 1
FAR = (2, 1, 3, 0)
PLANE = sorted(
    [(dx, dy) for dx in range(RING) for dy in range(RING)],
    key=lambda o: -min(o[0], RING - o[0]) - min(o[1], RING - o[1]),
)


def kernel(
    hidden,
    keys,
    vals,
    lens,
    ids,
    guid,
    wq,
    kvw,
    wo,
    gain,
    wh,
    out,
    h_c,
    wq_v,
    kvw_v,
    kv_v,
    k_v,
    v_v,
    wo_v,
    wh_v,
    ids_v,
    gain_all,
    part,
    recv_b,
    q_s,
    att_s,
    att_b,
    att_all,
    part_d,
    recv_d,
    resid,
    buf,
    acc,
    ssq,
    counts,
    gcol,
    tot_one,
    tot_all,
    hid_v,
    gain_v,
    lens_v,
    guid_v,
    load_sem,
    w_recv,
    z_recv,
    c_recv,
    f_recv,
    sib_recv,
    one,
):
    S = lax.axis_index("stream")
    D = lax.axis_index("dp")
    T = lax.axis_index("tensor")
    zl, c = T // 2, T % 2
    x, y = D // RING, D % RING
    sib = (S, D, zl * 2 + 1 - c)
    names = ("w", "a", "gain", "b", "c", "d", "z", "f", "sib", "t")
    send_of = {name: one.at[n] for n, name in enumerate(names)}
    recv_of = {name: one.at[len(names) + n] for n, name in enumerate(names)}

    def remote(src, dst, ssem, rsem, dev):
        copy = pltpu.make_async_remote_copy(
            src_ref=src,
            dst_ref=dst,
            send_sem=ssem,
            recv_sem=rsem,
            device_id=dev,
            device_id_type=MESH,
        )
        copy.start()

    def arrived(ref, rsem):
        pltpu.make_async_remote_copy(
            src_ref=ref,
            dst_ref=ref,
            send_sem=send_of["w"],
            recv_sem=rsem,
            device_id=sib,
            device_id_type=MESH,
        ).wait_recv()

    def left(ref, name):
        pltpu.make_async_remote_copy(
            src_ref=ref,
            dst_ref=ref,
            send_sem=send_of[name],
            recv_sem=recv_of[name],
            device_id=sib,
            device_id_type=MESH,
        ).wait_send()

    def peer(dx, dy):
        return ((x + dx) % RING) * RING + (y + dy) % RING

    mark("p00_entry")
    barrier = pltpu.get_barrier_semaphore()

    def greet(dev):
        pl.semaphore_signal(barrier, inc=1, device_id=dev, device_id_type=MESH)

    for t in range(TEN):
        greet((1 - S, D, t))
    for dx, dy in PLANE[:-1]:
        greet((S, peer(dx, dy), T))
        greet((S, peer(dx, dy), zl * 2 + 1 - c))
    for i in range(1, TEN):
        greet((S, D, (T + i) % TEN))

    loads = []

    def load(src, dst, sem=None):
        if sem is None:
            sem = load_sem.at[len(loads)]
            loads.append(sem)
        copy = pltpu.make_async_copy(src, dst, sem)
        copy.start()
        return copy

    l_hid = load(hidden.at[0], hid_v)
    load(hidden.at[0, pl.ds(c * 16, 16)], h_c.at[T], recv_of["a"])
    l_gain = load(gain, gain_v)
    l_lens = load(lens, lens_v)
    l_guid = load(guid, guid_v)
    l_wq = load(wq, wq_v.at[c])
    l_kv = load(kvw, kvw_v)
    for g in range(8):
        load(
            ids.at[pl.ds(S * 128 + PLACE[g] * 16, 16), :],
            ids_v.at[pl.ds(g * 16, 16), :],
            load_sem.at[12],
        )
    l_k = load(keys.at[0, :, 0], k_v)
    l_v = load(vals.at[0, :, 0], v_v)
    l_wo = load(wo, wo_v.at[c])
    l_hid.wait()
    pl.semaphore_wait(barrier, 45)

    mark("p01_hidden")
    for dz in (3, 2, 1):
        for core in (0, 1):
            dev = (S, D, ((zl + dz) % 4) * 2 + core)
            remote(
                hid_v.at[pl.ds(core * 16, 16)], h_c.at[T], send_of["a"], recv_of["a"], dev
            )
    remote(hid_v.at[pl.ds(16 - c * 16, 16)], h_c.at[T], send_of["a"], recv_of["a"], sib)
    remote(wq, wq_v.at[c], send_of["w"], w_recv.at[0], sib)
    l_gain.wait()
    gain_all[D] = gain_v[...].astype(F32).reshape(1, 512)
    l_wh = load(wh, wh_v)
    remote(wo, wo_v.at[c], send_of["w"], w_recv.at[2], sib)
    l_kv.wait()
    for n in range(2):
        kv_v[c, :, n * 128 : (n + 1) * 128] = kvw_v[:, n, :]
    l_wq.wait()
    remote(kv_v.at[c], kv_v.at[c], send_of["w"], w_recv.at[1], sib)
    arrived(h_c, recv_of["a"])

    mark("p02_qkv")
    h = h_c[...].reshape(128, 512)
    for i in range(2):
        g = (c + i) % 2
        if i == 1:
            arrived(wq_v.at[g], w_recv.at[0])
            arrived(kv_v.at[g], w_recv.at[1])
        for n in range(4):
            cols = pl.ds(n * 256, 256)
            r = jnp.dot(h, wq_v[g, :, cols], preferred_element_type=F32)
            part[:, g, :, cols] = r.reshape(8, 16, 256).astype(BF16)
        r = jnp.dot(h, kv_v[g], preferred_element_type=F32)
        part[:, g, :, pl.ds(1024, 256)] = r.reshape(8, 16, 256).astype(BF16)
        for n in range(8):
            to = peer(FAR[n // 2], (y + c) % 2 + 2 - 2 * (n % 2))
            k = to // 2
            if i == 1:
                remote(
                    part.at[k, g], recv_b.at[D], send_of["b"], recv_of["b"], (S, to, zl * 2 + g)
                )
                continue

            @pl.when(to == D)
            def _():
                pltpu.make_async_copy(part.at[k, g], recv_b.at[D], recv_of["b"]).start()

            @pl.when(to != D)
            def _():
                remote(
                    part.at[k, g], recv_b.at[D], send_of["b"], recv_of["b"], (S, to, zl * 2 + g)
                )
    for i in range(1, DP):
        to = (D + i) % DP
        remote(gain_all.at[D], gain_all.at[D], send_of["gain"], recv_of["gain"], (S, to, T))

    mark("p03_tables")
    lane = lax.broadcasted_iota(jnp.int32, (16, HEAD), 1)
    row = lax.broadcasted_iota(jnp.int32, (16, HEAD), 0)
    freq = jnp.exp(((lane % 64).astype(F32) * (2.0 / HEAD)) * (-jnp.log(F32(rope_theta))))
    l_lens.wait()
    l_guid.wait()
    position = jnp.zeros((16, HEAD), jnp.int32)
    for p in range(16):
        position = jnp.where(row == p, lens_v[0, p], position)
    angle = position.astype(F32) * freq
    cosine = jnp.cos(angle)
    sine = jnp.sin(angle) * jnp.where(lane < 64, -1.0, 1.0)

    pltpu.make_async_copy(ids.at[pl.ds(0, 128), :], ids_v, load_sem.at[12]).wait()
    base = (D * TEN + T) * 512
    ids_v[...] = jnp.transpose(ids_v[...]) - base
    for n in range(4):
        column = lax.broadcasted_iota(jnp.int32, (128, 128), 0) + n * 128

        def add(r, total):
            for k in range(8):
                here = ids_v[pl.ds(r * 8 + k, 1), :]
                total = total + jnp.where(column == here, 1.0, 0.0)
            return total

        total = lax.fori_loop(0, 16, add, jnp.zeros((128, 128), F32))
        counts[:, pl.ds(n * 128, 128)] = jnp.transpose(total) * penalty_step
    guide = jnp.transpose(jnp.broadcast_to(guid_v[pl.ds(S, 1), :], (128, 128)))
    for g in range(8):
        gcol[g * 16 : (g + 1) * 16] = guide[PLACE[g] * 16 : (PLACE[g] + 1) * 16]

    mark("p04_sumwait")
    arrived(recv_b, recv_of["b"])
    qkv = recv_b[0].astype(F32)
    for i in range(1, DP):
        qkv = qkv + recv_b[i].astype(F32)

    mark("p05_rope")

    def turn(v):
        return v * cosine + pltpu.roll(v, 64, 1) * sine

    for g in range(8):
        q_s[:, g, :] = turn(qkv[:, g * HEAD : (g + 1) * HEAD])
    k_new = turn(qkv[:, 1024:1152]).astype(BF16).astype(F32)
    v_new = qkv[:, 1152:1280].astype(BF16).astype(F32)

    mark("p06_attn")
    l_k.wait()
    l_v.wait()
    scale = HEAD ** (-0.5)
    slot_at = lax.broadcasted_iota(jnp.int32, (8, 256), 1)
    for start in (0, 8):
        prompts = range(start, start + 8)
        q = [q_s[p].astype(BF16) for p in prompts]
        scores = [
            lax.dot_general(
                q[p - start], k_v[p], (((1,), (1,)), ((), ())), preferred_element_type=F32
            )
            for p in prompts
        ]
        k_own = jnp.concatenate([jnp.broadcast_to(k_new[p : p + 1], (8, HEAD)) for p in prompts])
        v_own = jnp.concatenate([jnp.broadcast_to(v_new[p : p + 1], (8, HEAD)) for p in prompts])
        q_all = jnp.concatenate([v.astype(F32) for v in q])
        e_own = jnp.exp(jnp.sum(q_all * k_own, axis=1, keepdims=True) * scale)
        e = jnp.concatenate(
            [
                jnp.where(slot_at < lens_v[0, p], jnp.exp(scores[p - start] * scale), 0.0)
                for p in prompts
            ]
        )
        den = jnp.sum(e, axis=1, keepdims=True) + e_own
        w = (e / den).astype(BF16)
        w_own = (e_own / den).astype(BF16).astype(F32)
        o = jnp.concatenate(
            [
                jnp.dot(
                    w[(p - start) * 8 : (p - start + 1) * 8],
                    v_v[p],
                    preferred_element_type=F32,
                )
                for p in prompts
            ]
        )
        att_s[pl.ds(start, 8)] = (o + w_own * v_own).reshape(8, 8, HEAD)
    for g in range(8):
        att_b[:, pl.ds(g * HEAD, HEAD)] = att_s[:, g, :].astype(BF16)

    mark("p07_gatherC")
    core = D % 2
    slot = c * 8 + D // 2
    for dx, dy in PLANE:
        if (dx, dy) != (0, 0):
            to = peer(dx, dy)
            remote(att_b, att_all.at[slot], send_of["c"], c_recv.at[x], (S, to, zl * 2 + core))

    @pl.when(core == c)
    def _():
        pltpu.make_async_copy(att_b, att_all.at[slot], c_recv.at[x]).start()

    @pl.when(core != c)
    def _():
        remote(att_b, att_all.at[slot], send_of["c"], c_recv.at[x], sib)

    l_wo.wait()
    arrived(wo_v.at[1 - c], w_recv.at[2])

    for pair in ((2, 1), (3, 0)):
        blocks = [(x + dx) % RING for dx in pair]
        for block in blocks:
            arrived(att_all.at[pl.ds(0, 4)], c_recv.at[block])
        mark(f"p08_outproj{pair[0]}")
        a0 = jnp.concatenate([att_all[pl.ds(2 * b, 2)].reshape(32, 1024) for b in blocks])
        a1 = jnp.concatenate([att_all[pl.ds(8 + 2 * b, 2)].reshape(32, 1024) for b in blocks])
        for n in range(2):
            cols = pl.ds(n * 256, 256)
            r = jnp.dot(a0, wo_v[0, :, cols], preferred_element_type=F32)
            r = r + jnp.dot(a1, wo_v[1, :, cols], preferred_element_type=F32)
            for m, block in enumerate(blocks):
                part_d[block, :, cols] = r[m * 32 : (m + 1) * 32].astype(BF16)
        for block in blocks:
            other = (block // 2 - S) * (block // 2 - S)
            to = (1 - other) * (1 + block % 2) + other * 3 * (block % 2)

            @pl.when(to != zl)
            def _():
                remote(
                    part_d.at[block],
                    recv_d.at[(zl - to + 3) % 4],
                    send_of["d"],
                    recv_of["d"],
                    (S, D, to * 2 + c),
                )
        mark(f"p08b_wait{pair[0]}")

    def owned(z):
        inner = ((z + 1) // 2) % 2
        half = inner * S + (1 - inner) * (1 - S)
        return half, 2 * half + inner * (z - 1) + (1 - inner) * (z // 3)

    mark("p09_sumwaitD")
    my_half, mine = owned(zl)
    my_j = 2 * (mine % 2) + c
    total = h_c[pl.ds(2 * mine, 2)].reshape(32, 512).astype(F32) + part_d[mine].astype(F32)
    arrived(recv_d, recv_of["d"])
    for i in range(3):
        total = total + recv_d[i].astype(F32)
    resid[...] = total.astype(BF16)

    mark("p10_z")
    place = buf.at[S, D, pl.ds(my_j * 32, 32), :]
    for z in range(4):
        at_home = jnp.logical_and(my_half == S, 2 * z + S == T)

        @pl.when(at_home)
        def _():
            pltpu.make_async_copy(resid, place, z_recv.at[my_j]).start()

        @pl.when(jnp.logical_not(at_home))
        def _():
            remote(resid, place, send_of["z"], z_recv.at[my_j], (my_half, D, 2 * z + S))

    arrived(gain_all.at[pl.ds(0, DP - 1)], recv_of["gain"])
    l_wh.wait()
    acc[...] = jnp.zeros_like(acc)
    ssq[...] = jnp.zeros_like(ssq)

    def neighbour(name, step):
        if name == "x":
            return (S, ((x + RING + step) % RING) * RING + y, T)
        return (S, x * RING + (y + RING + step) % RING, T)

    def slot_of(dx, dy):
        return ((x + RING - dx) % RING) * RING + (y + RING - dy) % RING

    def send_on(piece, hops):
        slot, quarter = slot_of(*piece[:2]), piece[2]
        rows = buf.at[c, slot, pl.ds(quarter * 32, 32), :]
        for hop in hops:
            remote(rows, rows, send_of["f"], f_recv.at[SEM[onward(piece, hop)]], neighbour(*hop))

    def share(dx, dy):
        whole = buf.at[c, slot_of(dx, dy)]
        remote(whole, whole, send_of["sib"], sib_recv.at[slot_of(dx, dy)], sib)

    def head(dx, dy):
        slot = slot_of(dx, dy)
        arrived(buf.at[1 - c, slot], sib_recv.at[slot])
        v = buf[:, slot].reshape(256, 512).astype(F32)
        v2 = v * v
        ssq[...] += v2[:, 0:128] + v2[:, 128:256] + v2[:, 256:384] + v2[:, 384:512]
        w = (v * gain_all[slot]).astype(BF16)
        acc[...] += jnp.dot(
            w,
            wh_v[pl.ds(pl.multiple_of(slot * 512, 512), 512), :],
            preferred_element_type=F32,
        )

    mark("p10b_zwait")
    for quarter in range(4):
        arrived(buf.at[c, D, pl.ds(quarter * 32, 32), :], z_recv.at[quarter])
        send_on((0, 0, quarter), HOPS[(0, 0, quarter)][:2])
    mark("p11_own")
    for quarter in range(4):
        send_on((0, 0, quarter), HOPS[(0, 0, quarter)][2:])
    share(0, 0)
    complete = [(0, (0, 0))]
    held, leaves = {}, {}
    for n, piece in enumerate(ORDER):
        if n % 10 == 0:
            mark(f"p12_pieces{n:02d}")
        dx, dy, quarter = piece
        slot = slot_of(dx, dy)
        if HOPS[piece]:
            arrived(buf.at[c, slot, pl.ds(quarter * 32, 32), :], f_recv.at[SEM[piece]])
            send_on(piece, forwards(piece))
        else:
            leaves[dx, dy] = leaves.get((dx, dy), 0) + 1
            if leaves[dx, dy] == LEAVES[dx, dy]:
                arrived(buf.at[c, slot, pl.ds(0, 32 * LEAVES[dx, dy]), :], f_recv.at[SEM[piece]])
        held[dx, dy] = held.get((dx, dy), 0) + 1
        if held[dx, dy] == 4:
            share(dx, dy)
            complete.append((n, (dx, dy)))
        if complete and n - complete[0][0] >= 8:
            head(*complete.pop(0)[1])
    mark("p13_lastheads")
    for _, offset in complete:
        head(*offset)

    mark("p16_guided")
    inv = lax.rsqrt(jnp.sum(ssq[...], axis=1, keepdims=True) / WIDTH + norm_eps)
    cond = acc[0:128, :] * inv[0:128]
    uncond = acc[128:256, :] * inv[128:256]
    guide = gcol[:, 0:1]
    guided = uncond + guide * (cond - uncond) - counts[...]
    acc[0:128, :] = guided
    e = jnp.exp(guided)
    e = e[:, 0:128] + e[:, 128:256] + e[:, 256:384] + e[:, 384:512]
    mark("p17_total")
    tot_one[...] = jnp.sum(jnp.transpose(e), axis=0, keepdims=True)

    for n, (dx, dy) in enumerate(PLANE):
        for dt in range(TEN):
            if (dx, dy, dt) != (0, 0, 0):
                to = (S, peer(dx, dy), (T + dt) % TEN)
                remote(tot_one, tot_all.at[n * TEN + dt - n // 15], send_of["t"], recv_of["t"], to)
    arrived(tot_all, recv_of["t"])
    mark("p18_out")
    totals = tot_one[...] + jnp.sum(tot_all[...], axis=0)
    log_total = jnp.transpose(jnp.broadcast_to(jnp.log(totals), (128, 128)))
    for g in range(8):
        for n in range(4):
            cols = pl.ds(n * 128, 128)
            out[pl.ds(PLACE[g] * 16, 16), cols] = (
                acc[pl.ds(g * 16, 16), cols] - log_total[g * 16 : (g + 1) * 16]
            )

    mark("p19_waitsend")
    left(wq_v.at[0], "w")
    left(kv_v.at[0], "w")
    left(wo_v.at[0], "w")
    left(h_c.at[pl.ds(0, 7)], "a")
    left(gain_all.at[pl.ds(0, DP - 1)], "gain")
    left(part_d.at[pl.ds(0, 3)], "d")
    left(buf.at[0, pl.ds(0, 15)], "f")
    left(buf.at[0], "sib")
    left(tot_all, "t")
    kept_c = core == c
    kept_z = jnp.logical_and(my_half == S, c == S)

    @pl.when(kept_c)
    def _():
        left(recv_b.at[pl.ds(0, DP - 1)], "b")
        left(att_all.at[pl.ds(0, DP - 1)], "c")

    @pl.when(jnp.logical_not(kept_c))
    def _():
        left(recv_b, "b")
        left(att_all, "c")

    @pl.when(kept_z)
    def _():
        left(part_d.at[pl.ds(0, 3)], "z")

    @pl.when(jnp.logical_not(kept_z))
    def _():
        left(part_d, "z")

    mark(None)


def body(hidden, keys, vals, lens, ids, guid, wq, kvw, wo, gain, wh):
    dma = pltpu.SemaphoreType.DMA
    anywhere = pl.BlockSpec(memory_space=pl.ANY)
    vmem = pl.BlockSpec(memory_space=pltpu.VMEM)
    return pl.pallas_call(
        kernel,
        out_shape=pltpu.VMEM((128, 512), F32),
        in_specs=[anywhere] * 11,
        out_specs=vmem,
        scratch_shapes=[
            pltpu.VMEM((TEN, 16, 512), BF16),
            pltpu.VMEM((2, 512, 1024), BF16),
            pltpu.VMEM((512, 2, 128), BF16),
            pltpu.VMEM((2, 512, 256), BF16),
            pltpu.VMEM((16, 256, 128), BF16),
            pltpu.VMEM((16, 256, 128), BF16),
            pltpu.VMEM((2, 1024, 512), BF16),
            pltpu.VMEM((8192, 512), BF16),
            pltpu.VMEM((128, 128), jnp.int32),
            pltpu.VMEM((DP, 1, 512), F32),
            pltpu.VMEM((8, 2, 16, 1280), BF16),
            pltpu.VMEM((DP, 16, 1280), BF16),
            pltpu.VMEM((16, 8, 128), F32),
            pltpu.VMEM((16, 8, 128), F32),
            pltpu.VMEM((16, 1024), BF16),
            pltpu.VMEM((DP, 16, 1024), BF16),
            pltpu.VMEM((4, 32, 512), BF16),
            pltpu.VMEM((3, 32, 512), BF16),
            pltpu.VMEM((32, 512), BF16),
            pltpu.VMEM((2, DP, 128, 512), BF16),
            pltpu.VMEM((256, 512), F32),
            pltpu.VMEM((256, 128), F32),
            pltpu.VMEM((128, 512), F32),
            pltpu.VMEM((128, 128), F32),
            pltpu.VMEM((1, 128), F32),
            pltpu.VMEM((DP * TEN - 1, 1, 128), F32),
            pltpu.VMEM((32, 512), BF16),
            pltpu.VMEM((512,), BF16),
            pltpu.SMEM((1, 16), jnp.int32),
            pltpu.VMEM((2, 128), F32),
            dma((13,)),
            dma((3,)),
            dma((4,)),
            dma((4,)),
            dma((N_SEM,)),
            dma((DP,)),
            dma((20,)),
        ],
        compiler_params=pltpu.CompilerParams(
            collective_id=0, has_side_effects=True, vmem_limit_bytes=60 * 1024 * 1024
        ),
    )(hidden, keys, vals, lens, ids, guid.reshape(2, 128), wq, kvw, wo, gain, wh)


def solution(mesh):
    return jax.shard_map(
        body,
        mesh=mesh,
        in_specs=(
            P("stream", "tensor", "dp"),
            P("stream", "dp", "tensor", None, None),
            P("stream", "dp", "tensor", None, None),
            P("stream", "dp"),
            P(),
            P(),
            P("dp", "tensor"),
            P("dp", None, "tensor"),
            P("tensor", "dp"),
            P("dp"),
            P(None, ("dp", "tensor")),
        ),
        out_specs=P("stream", ("dp", "tensor")),
        check_vma=False,
    )
```

```python
import heapq

import jax
import jax.numpy as jnp
from jax import lax
from jax.experimental import pallas as pl
from jax.experimental.pallas import tpu as pltpu
from jax.sharding import PartitionSpec as P

MESH = pl.DeviceIdType.MESH
F32 = jnp.float32
BF16 = jnp.bfloat16
WIDTH = 8192
HEAD = 128
RING = 4
DP = 16
TEN = 8

rope_theta = 500000.0
penalty_step = 1.5
norm_eps = 1e-05


MARKS = False
open_scope = []


def mark(name):
    if MARKS:
        if open_scope:
            open_scope.pop().__exit__(None, None, None)
        if name:
            open_scope.append(jax.named_scope(name))
            open_scope[0].__enter__()


def routes():
    found = []
    for depth in range(5):
        for dx in range(RING):
            for dy in range(RING):
                if min(dx, RING - dx) + min(dy, RING - dy) != depth:
                    continue
                for quarter in range(4):
                    first, second = (dx, dy) if quarter < 2 else (dy, dx)
                    names = ("x", "y") if quarter < 2 else ("y", "x")
                    odd = quarter % 2
                    hops = []
                    if second == 0:
                        if first == 0:
                            hops += [(names[0], 1), (names[0], -1)]
                        elif first == 1 and not odd:
                            hops += [(names[0], 1)]
                        elif first == 3 and odd:
                            hops += [(names[0], -1)]
                        hops += [(names[1], 1), (names[1], -1)]
                    elif second == 1 and not odd:
                        hops += [(names[1], 1)]
                    elif second == 3 and odd:
                        hops += [(names[1], -1)]
                    found.append((depth, dx, dy, quarter, hops))
    return found


HOPS = {r[1:4]: r[4] for r in routes()}
N_FORWARD = sum(len(hops) for hops in HOPS.values())
PLACE = [4 * (g // 4) + 2 * (g % 2) + (g // 2) % 2 for g in range(8)]


def onward(piece, hop):
    dx, dy, quarter = piece
    axis, step = hop
    if axis == "x":
        return (dx + step) % RING, dy, quarter
    return dx, (dy + step) % RING, quarter


def further(piece):
    return max([1 + further(onward(piece, hop)) for hop in HOPS[piece]], default=0)


def forwards(piece):
    return sorted(HOPS[piece], key=lambda hop: -further(onward(piece, hop)))


def plan():
    free, arrivals, order = {}, [], []

    def send(piece, hop, now):
        free[hop] = max(free.get(hop, 0.0), now) + 0.7
        heapq.heappush(arrivals, (free[hop] + 1.66, len(order), onward(piece, hop)))

    own = [(0, 0, quarter) for quarter in range(4)]
    first = [(piece, hop) for piece in own for hop in HOPS[piece][:2]]
    first += [(piece, hop) for piece in own for hop in HOPS[piece][2:]]
    for piece, hop in first:
        send(piece, hop, 0.0)
    now = 0.0
    while arrivals:
        when, _, piece = heapq.heappop(arrivals)
        now = max(now, when) + 0.02
        order.append(piece)
        for hop in forwards(piece):
            send(piece, hop, now)
    return order


ORDER = plan()


def semaphores():
    number = {}
    keys = [piece if HOPS[piece] else piece[:2] for piece in ORDER]
    for key in keys:
        number.setdefault(key, len(number))
    return {piece: number[key] for piece, key in zip(ORDER, keys)}, len(number)


SEM, N_SEM = semaphores()
LEAVES = {}
for leaf in ORDER:
    if not HOPS[leaf]:
        LEAVES[leaf[:2]] = LEAVES.get(leaf[:2], 0) + 1
FAR = (2, 1, 3, 0)
PLANE = sorted(
    [(dx, dy) for dx in range(RING) for dy in range(RING)],
    key=lambda o: -min(o[0], RING - o[0]) - min(o[1], RING - o[1]),
)


def kernel(
    hidden,
    keys,
    vals,
    lens,
    ids,
    guid,
    wq,
    kvw,
    wo,
    gain,
    wh,
    out,
    h_c,
    wq_v,
    kvw_v,
    kv_v,
    k_v,
    v_v,
    wo_v,
    wh_v,
    ids_v,
    gain_all,
    part,
    recv_b,
    q_s,
    att_s,
    att_b,
    att_all,
    part_d,
    recv_d,
    resid,
    buf,
    acc,
    ssq,
    counts,
    gcol,
    tot_one,
    tot_all,
    hid_v,
    gain_v,
    lens_v,
    guid_v,
    load_sem,
    w_recv,
    z_recv,
    c_recv,
    f_recv,
    sib_recv,
    one,
):
    S = lax.axis_index("stream")
    D = lax.axis_index("dp")
    T = lax.axis_index("tensor")
    zl, c = T // 2, T % 2
    x, y = D // RING, D % RING
    sib = (S, D, zl * 2 + 1 - c)
    names = ("a", "gain", "b", "c", "d", "t")
    recv_of = {name: one.at[n] for n, name in enumerate(names)}
    departed = one.at[len(names)]

    def remote(src, dst, ssem, rsem, dev):
        copy = pltpu.make_async_remote_copy(
            src_ref=src,
            dst_ref=dst,
            send_sem=ssem,
            recv_sem=rsem,
            device_id=dev,
            device_id_type=MESH,
        )
        copy.start()

    def arrived(ref, rsem):
        pltpu.make_async_remote_copy(
            src_ref=ref,
            dst_ref=ref,
            send_sem=departed,
            recv_sem=rsem,
            device_id=sib,
            device_id_type=MESH,
        ).wait_recv()

    def left(ref):
        pltpu.make_async_remote_copy(
            src_ref=ref,
            dst_ref=ref,
            send_sem=departed,
            recv_sem=recv_of["a"],
            device_id=sib,
            device_id_type=MESH,
        ).wait_send()

    def peer(dx, dy):
        return ((x + dx) % RING) * RING + (y + dy) % RING

    mark("p00_entry")
    barrier = pltpu.get_barrier_semaphore()

    def greet(dev):
        pl.semaphore_signal(barrier, inc=1, device_id=dev, device_id_type=MESH)

    for t in range(TEN):
        greet((1 - S, D, t))
    for dx, dy in PLANE[:-1]:
        greet((S, peer(dx, dy), T))
        greet((S, peer(dx, dy), zl * 2 + 1 - c))
    for i in range(1, TEN):
        greet((S, D, (T + i) % TEN))

    loads = []

    def load(src, dst, sem=None):
        if sem is None:
            sem = load_sem.at[len(loads)]
            loads.append(sem)
        copy = pltpu.make_async_copy(src, dst, sem)
        copy.start()
        return copy

    l_hid = load(hidden.at[0], hid_v)
    load(hidden.at[0, pl.ds(c * 16, 16)], h_c.at[T], recv_of["a"])
    l_gain = load(gain, gain_v)
    l_lens = load(lens, lens_v)
    l_guid = load(guid, guid_v)
    l_wq = load(wq, wq_v.at[c])
    l_kv = load(kvw, kvw_v)
    for g in range(8):
        load(
            ids.at[pl.ds(S * 128 + PLACE[g] * 16, 16), :],
            ids_v.at[pl.ds(g * 16, 16), :],
            load_sem.at[12],
        )
    l_k = load(keys.at[0, :, 0], k_v)
    l_v = load(vals.at[0, :, 0], v_v)
    l_wo = load(wo, wo_v.at[c])
    l_hid.wait()
    pl.semaphore_wait(barrier, 45)

    mark("p01_hidden")
    for dz in (3, 2, 1):
        for core in (0, 1):
            dev = (S, D, ((zl + dz) % 4) * 2 + core)
            remote(
                hid_v.at[pl.ds(core * 16, 16)], h_c.at[T], departed, recv_of["a"], dev
            )
    remote(hid_v.at[pl.ds(16 - c * 16, 16)], h_c.at[T], departed, recv_of["a"], sib)
    remote(wq, wq_v.at[c], departed, w_recv.at[0], sib)
    l_gain.wait()
    gain_all[D] = gain_v[...].astype(F32).reshape(1, 512)
    l_wh = load(wh, wh_v)
    remote(wo, wo_v.at[c], departed, w_recv.at[2], sib)
    l_kv.wait()
    for n in range(2):
        kv_v[c, :, n * 128 : (n + 1) * 128] = kvw_v[:, n, :]
    l_wq.wait()
    remote(kv_v.at[c], kv_v.at[c], departed, w_recv.at[1], sib)
    arrived(h_c, recv_of["a"])

    mark("p02_qkv")
    h = h_c[...].reshape(128, 512)
    for i in range(2):
        g = (c + i) % 2
        if i == 1:
            arrived(wq_v.at[g], w_recv.at[0])
            arrived(kv_v.at[g], w_recv.at[1])
        for n in range(4):
            cols = pl.ds(n * 256, 256)
            r = jnp.dot(h, wq_v[g, :, cols], preferred_element_type=F32)
            part[:, g, :, cols] = r.reshape(8, 16, 256).astype(BF16)
        r = jnp.dot(h, kv_v[g], preferred_element_type=F32)
        part[:, g, :, pl.ds(1024, 256)] = r.reshape(8, 16, 256).astype(BF16)
        for n in range(8):
            to = peer(FAR[n // 2], (y + c) % 2 + 2 - 2 * (n % 2))
            k = to // 2
            if i == 1:
                remote(
                    part.at[k, g], recv_b.at[D], departed, recv_of["b"], (S, to, zl * 2 + g)
                )
                continue

            @pl.when(to == D)
            def _():
                pltpu.make_async_copy(part.at[k, g], recv_b.at[D], recv_of["b"]).start()

            @pl.when(to != D)
            def _():
                remote(
                    part.at[k, g], recv_b.at[D], departed, recv_of["b"], (S, to, zl * 2 + g)
                )
    for i in range(1, DP):
        to = (D + i) % DP
        remote(gain_all.at[D], gain_all.at[D], departed, recv_of["gain"], (S, to, T))

    mark("p03_tables")
    lane = lax.broadcasted_iota(jnp.int32, (16, HEAD), 1)
    row = lax.broadcasted_iota(jnp.int32, (16, HEAD), 0)
    freq = jnp.exp(((lane % 64).astype(F32) * (2.0 / HEAD)) * (-jnp.log(F32(rope_theta))))
    l_lens.wait()
    l_guid.wait()
    position = jnp.zeros((16, HEAD), jnp.int32)
    for p in range(16):
        position = jnp.where(row == p, lens_v[0, p], position)
    angle = position.astype(F32) * freq
    cosine = jnp.cos(angle)
    sine = jnp.sin(angle) * jnp.where(lane < 64, -1.0, 1.0)

    pltpu.make_async_copy(ids.at[pl.ds(0, 128), :], ids_v, load_sem.at[12]).wait()
    base = (D * TEN + T) * 512
    ids_v[...] = jnp.transpose(ids_v[...]) - base
    for n in range(4):
        column = lax.broadcasted_iota(jnp.int32, (128, 128), 0) + n * 128

        def add(r, total):
            for k in range(8):
                here = ids_v[pl.ds(r * 8 + k, 1), :]
                total = total + jnp.where(column == here, 1.0, 0.0)
            return total

        total = lax.fori_loop(0, 16, add, jnp.zeros((128, 128), F32))
        counts[:, pl.ds(n * 128, 128)] = jnp.transpose(total) * penalty_step
    guide = jnp.transpose(jnp.broadcast_to(guid_v[pl.ds(S, 1), :], (128, 128)))
    for g in range(8):
        gcol[g * 16 : (g + 1) * 16] = guide[PLACE[g] * 16 : (PLACE[g] + 1) * 16]

    mark("p04_sumwait")
    arrived(recv_b, recv_of["b"])
    qkv = recv_b[0].astype(F32)
    for i in range(1, DP):
        qkv = qkv + recv_b[i].astype(F32)

    mark("p05_rope")

    def turn(v):
        return v * cosine + pltpu.roll(v, 64, 1) * sine

    for g in range(8):
        q_s[:, g, :] = turn(qkv[:, g * HEAD : (g + 1) * HEAD])
    k_new = turn(qkv[:, 1024:1152]).astype(BF16).astype(F32)
    v_new = qkv[:, 1152:1280].astype(BF16).astype(F32)

    mark("p06_attn")
    l_k.wait()
    l_v.wait()
    scale = HEAD ** (-0.5)
    slot_at = lax.broadcasted_iota(jnp.int32, (8, 256), 1)
    for start in (0, 8):
        prompts = range(start, start + 8)
        q = [q_s[p].astype(BF16) for p in prompts]
        scores = [
            lax.dot_general(
                q[p - start], k_v[p], (((1,), (1,)), ((), ())), preferred_element_type=F32
            )
            for p in prompts
        ]
        k_own = jnp.concatenate([jnp.broadcast_to(k_new[p : p + 1], (8, HEAD)) for p in prompts])
        v_own = jnp.concatenate([jnp.broadcast_to(v_new[p : p + 1], (8, HEAD)) for p in prompts])
        q_all = jnp.concatenate([v.astype(F32) for v in q])
        e_own = jnp.exp(jnp.sum(q_all * k_own, axis=1, keepdims=True) * scale)
        e = jnp.concatenate(
            [
                jnp.where(slot_at < lens_v[0, p], jnp.exp(scores[p - start] * scale), 0.0)
                for p in prompts
            ]
        )
        den = jnp.sum(e, axis=1, keepdims=True) + e_own
        w = (e / den).astype(BF16)
        w_own = (e_own / den).astype(BF16).astype(F32)
        o = jnp.concatenate(
            [
                jnp.dot(
                    w[(p - start) * 8 : (p - start + 1) * 8],
                    v_v[p],
                    preferred_element_type=F32,
                )
                for p in prompts
            ]
        )
        att_s[pl.ds(start, 8)] = (o + w_own * v_own).reshape(8, 8, HEAD)
    for g in range(8):
        att_b[:, pl.ds(g * HEAD, HEAD)] = att_s[:, g, :].astype(BF16)

    mark("p07_gatherC")
    core = D % 2
    slot = c * 8 + D // 2
    for dx, dy in PLANE:
        if (dx, dy) != (0, 0):
            to = peer(dx, dy)
            remote(att_b, att_all.at[slot], departed, c_recv.at[x], (S, to, zl * 2 + core))

    @pl.when(core == c)
    def _():
        pltpu.make_async_copy(att_b, att_all.at[slot], c_recv.at[x]).start()

    @pl.when(core != c)
    def _():
        remote(att_b, att_all.at[slot], departed, c_recv.at[x], sib)

    l_wo.wait()
    arrived(wo_v.at[1 - c], w_recv.at[2])

    for pair in ((2, 1), (3, 0)):
        blocks = [(x + dx) % RING for dx in pair]
        for block in blocks:
            arrived(att_all.at[pl.ds(0, 4)], c_recv.at[block])
        mark(f"p08_outproj{pair[0]}")
        a0 = jnp.concatenate([att_all[pl.ds(2 * b, 2)].reshape(32, 1024) for b in blocks])
        a1 = jnp.concatenate([att_all[pl.ds(8 + 2 * b, 2)].reshape(32, 1024) for b in blocks])
        for n in range(2):
            cols = pl.ds(n * 256, 256)
            r = jnp.dot(a0, wo_v[0, :, cols], preferred_element_type=F32)
            r = r + jnp.dot(a1, wo_v[1, :, cols], preferred_element_type=F32)
            for m, block in enumerate(blocks):
                part_d[block, :, cols] = r[m * 32 : (m + 1) * 32].astype(BF16)
        for block in blocks:
            other = (block // 2 - S) * (block // 2 - S)
            to = (1 - other) * (1 + block % 2) + other * 3 * (block % 2)

            @pl.when(to != zl)
            def _():
                remote(
                    part_d.at[block],
                    recv_d.at[(zl - to + 3) % 4],
                    departed,
                    recv_of["d"],
                    (S, D, to * 2 + c),
                )
        mark(f"p08b_wait{pair[0]}")

    def owned(z):
        inner = ((z + 1) // 2) % 2
        half = inner * S + (1 - inner) * (1 - S)
        return half, 2 * half + inner * (z - 1) + (1 - inner) * (z // 3)

    mark("p09_sumwaitD")
    my_half, mine = owned(zl)
    my_j = 2 * (mine % 2) + c
    total = h_c[pl.ds(2 * mine, 2)].reshape(32, 512).astype(F32) + part_d[mine].astype(F32)
    arrived(recv_d, recv_of["d"])
    for i in range(3):
        total = total + recv_d[i].astype(F32)
    resid[...] = total.astype(BF16)

    mark("p10_z")
    place = buf.at[S, D, pl.ds(my_j * 32, 32), :]
    for z in range(4):
        at_home = jnp.logical_and(my_half == S, 2 * z + S == T)

        @pl.when(at_home)
        def _():
            pltpu.make_async_copy(resid, place, z_recv.at[my_j]).start()

        @pl.when(jnp.logical_not(at_home))
        def _():
            remote(resid, place, departed, z_recv.at[my_j], (my_half, D, 2 * z + S))

    arrived(gain_all.at[pl.ds(0, DP - 1)], recv_of["gain"])
    l_wh.wait()
    acc[...] = jnp.zeros_like(acc)
    ssq[...] = jnp.zeros_like(ssq)

    def neighbour(name, step):
        if name == "x":
            return (S, ((x + RING + step) % RING) * RING + y, T)
        return (S, x * RING + (y + RING + step) % RING, T)

    def slot_of(dx, dy):
        return ((x + RING - dx) % RING) * RING + (y + RING - dy) % RING

    def send_on(piece, hops):
        slot, quarter = slot_of(*piece[:2]), piece[2]
        rows = buf.at[c, slot, pl.ds(quarter * 32, 32), :]
        for hop in hops:
            remote(rows, rows, departed, f_recv.at[SEM[onward(piece, hop)]], neighbour(*hop))

    def share(dx, dy):
        whole = buf.at[c, slot_of(dx, dy)]
        remote(whole, whole, departed, sib_recv.at[slot_of(dx, dy)], sib)

    def head(dx, dy):
        slot = slot_of(dx, dy)
        arrived(buf.at[1 - c, slot], sib_recv.at[slot])
        v = buf[:, slot].reshape(256, 512).astype(F32)
        v2 = v * v
        ssq[...] += v2[:, 0:128] + v2[:, 128:256] + v2[:, 256:384] + v2[:, 384:512]
        w = (v * gain_all[slot]).astype(BF16)
        acc[...] += jnp.dot(
            w,
            wh_v[pl.ds(pl.multiple_of(slot * 512, 512), 512), :],
            preferred_element_type=F32,
        )

    mark("p10b_zwait")
    for quarter in range(4):
        arrived(buf.at[c, D, pl.ds(quarter * 32, 32), :], z_recv.at[quarter])
        send_on((0, 0, quarter), HOPS[(0, 0, quarter)][:2])
    mark("p11_own")
    for quarter in range(4):
        send_on((0, 0, quarter), HOPS[(0, 0, quarter)][2:])
    share(0, 0)
    complete = [(0, (0, 0))]
    held, leaves = {}, {}
    for n, piece in enumerate(ORDER):
        if n % 10 == 0:
            mark(f"p12_pieces{n:02d}")
        dx, dy, quarter = piece
        slot = slot_of(dx, dy)
        if HOPS[piece]:
            arrived(buf.at[c, slot, pl.ds(quarter * 32, 32), :], f_recv.at[SEM[piece]])
            send_on(piece, forwards(piece))
        else:
            leaves[dx, dy] = leaves.get((dx, dy), 0) + 1
            if leaves[dx, dy] == LEAVES[dx, dy]:
                arrived(buf.at[c, slot, pl.ds(0, 32 * LEAVES[dx, dy]), :], f_recv.at[SEM[piece]])
        held[dx, dy] = held.get((dx, dy), 0) + 1
        if held[dx, dy] == 4:
            share(dx, dy)
            complete.append((n, (dx, dy)))
        if complete and n - complete[0][0] >= 8:
            head(*complete.pop(0)[1])
    mark("p13_lastheads")
    for _, offset in complete:
        head(*offset)

    mark("p16_guided")
    inv = lax.rsqrt(jnp.sum(ssq[...], axis=1, keepdims=True) / WIDTH + norm_eps)
    cond = acc[0:128, :] * inv[0:128]
    uncond = acc[128:256, :] * inv[128:256]
    guide = gcol[:, 0:1]
    guided = uncond + guide * (cond - uncond) - counts[...]
    acc[0:128, :] = guided
    e = jnp.exp(guided)
    e = e[:, 0:128] + e[:, 128:256] + e[:, 256:384] + e[:, 384:512]
    mark("p17_total")
    tot_one[...] = jnp.sum(jnp.transpose(e), axis=0, keepdims=True)

    for n, (dx, dy) in enumerate(PLANE):
        for dt in range(TEN):
            if (dx, dy, dt) != (0, 0, 0):
                to = (S, peer(dx, dy), (T + dt) % TEN)
                remote(tot_one, tot_all.at[n * TEN + dt - n // 15], departed, recv_of["t"], to)
    arrived(tot_all, recv_of["t"])
    mark("p18_out")
    totals = tot_one[...] + jnp.sum(tot_all[...], axis=0)
    log_total = jnp.transpose(jnp.broadcast_to(jnp.log(totals), (128, 128)))
    for g in range(8):
        for n in range(4):
            cols = pl.ds(n * 128, 128)
            out[pl.ds(PLACE[g] * 16, 16), cols] = (
                acc[pl.ds(g * 16, 16), cols] - log_total[g * 16 : (g + 1) * 16]
            )

    mark("p19_waitsend")
    left(wq_v.at[0])
    left(kv_v.at[0])
    left(wo_v.at[0])
    left(h_c.at[pl.ds(0, 7)])
    left(gain_all.at[pl.ds(0, DP - 1)])
    left(part_d.at[pl.ds(0, 3)])
    left(buf.at[0, pl.ds(0, 15)])
    left(buf.at[0])
    left(tot_all)
    kept_c = core == c
    kept_z = jnp.logical_and(my_half == S, c == S)

    @pl.when(kept_c)
    def _():
        left(recv_b.at[pl.ds(0, DP - 1)])
        left(att_all.at[pl.ds(0, DP - 1)])

    @pl.when(jnp.logical_not(kept_c))
    def _():
        left(recv_b)
        left(att_all)

    @pl.when(kept_z)
    def _():
        left(part_d.at[pl.ds(0, 3)])

    @pl.when(jnp.logical_not(kept_z))
    def _():
        left(part_d)

    mark(None)


def body(hidden, keys, vals, lens, ids, guid, wq, kvw, wo, gain, wh):
    dma = pltpu.SemaphoreType.DMA
    anywhere = pl.BlockSpec(memory_space=pl.ANY)
    vmem = pl.BlockSpec(memory_space=pltpu.VMEM)
    return pl.pallas_call(
        kernel,
        out_shape=pltpu.VMEM((128, 512), F32),
        in_specs=[anywhere] * 11,
        out_specs=vmem,
        scratch_shapes=[
            pltpu.VMEM((TEN, 16, 512), BF16),
            pltpu.VMEM((2, 512, 1024), BF16),
            pltpu.VMEM((512, 2, 128), BF16),
            pltpu.VMEM((2, 512, 256), BF16),
            pltpu.VMEM((16, 256, 128), BF16),
            pltpu.VMEM((16, 256, 128), BF16),
            pltpu.VMEM((2, 1024, 512), BF16),
            pltpu.VMEM((8192, 512), BF16),
            pltpu.VMEM((128, 128), jnp.int32),
            pltpu.VMEM((DP, 1, 512), F32),
            pltpu.VMEM((8, 2, 16, 1280), BF16),
            pltpu.VMEM((DP, 16, 1280), BF16),
            pltpu.VMEM((16, 8, 128), F32),
            pltpu.VMEM((16, 8, 128), F32),
            pltpu.VMEM((16, 1024), BF16),
            pltpu.VMEM((DP, 16, 1024), BF16),
            pltpu.VMEM((4, 32, 512), BF16),
            pltpu.VMEM((3, 32, 512), BF16),
            pltpu.VMEM((32, 512), BF16),
            pltpu.VMEM((2, DP, 128, 512), BF16),
            pltpu.VMEM((256, 512), F32),
            pltpu.VMEM((256, 128), F32),
            pltpu.VMEM((128, 512), F32),
            pltpu.VMEM((128, 128), F32),
            pltpu.VMEM((1, 128), F32),
            pltpu.VMEM((DP * TEN - 1, 1, 128), F32),
            pltpu.VMEM((32, 512), BF16),
            pltpu.VMEM((512,), BF16),
            pltpu.SMEM((1, 16), jnp.int32),
            pltpu.VMEM((2, 128), F32),
            dma((13,)),
            dma((3,)),
            dma((4,)),
            dma((4,)),
            dma((N_SEM,)),
            dma((DP,)),
            dma((7,)),
        ],
        compiler_params=pltpu.CompilerParams(
            collective_id=0, has_side_effects=True, vmem_limit_bytes=60 * 1024 * 1024
        ),
    )(hidden, keys, vals, lens, ids, guid.reshape(2, 128), wq, kvw, wo, gain, wh)


def solution(mesh):
    return jax.shard_map(
        body,
        mesh=mesh,
        in_specs=(
            P("stream", "tensor", "dp"),
            P("stream", "dp", "tensor", None, None),
            P("stream", "dp", "tensor", None, None),
            P("stream", "dp"),
            P(),
            P(),
            P("dp", "tensor"),
            P("dp", None, "tensor"),
            P("tensor", "dp"),
            P("dp"),
            P(None, ("dp", "tensor")),
        ),
        out_specs=P("stream", ("dp", "tensor")),
        check_vma=False,
    )
```

```python
import heapq

import jax
import jax.numpy as jnp
from jax import lax
from jax.experimental import pallas as pl
from jax.experimental.pallas import tpu as pltpu
from jax.sharding import PartitionSpec as P

MESH = pl.DeviceIdType.MESH
F32 = jnp.float32
BF16 = jnp.bfloat16
WIDTH = 8192
HEAD = 128
RING = 4
DP = 16
TEN = 8

rope_theta = 500000.0
penalty_step = 1.5
norm_eps = 1e-05


MARKS = False
open_scope = []


def mark(name):
    if MARKS:
        if open_scope:
            open_scope.pop().__exit__(None, None, None)
        if name:
            open_scope.append(jax.named_scope(name))
            open_scope[0].__enter__()


def routes():
    found = []
    for depth in range(5):
        for dx in range(RING):
            for dy in range(RING):
                if min(dx, RING - dx) + min(dy, RING - dy) != depth:
                    continue
                for quarter in range(4):
                    first, second = (dx, dy) if quarter < 2 else (dy, dx)
                    names = ("x", "y") if quarter < 2 else ("y", "x")
                    odd = quarter % 2
                    hops = []
                    if second == 0:
                        if first == 0:
                            hops += [(names[0], 1), (names[0], -1)]
                        elif first == 1 and not odd:
                            hops += [(names[0], 1)]
                        elif first == 3 and odd:
                            hops += [(names[0], -1)]
                        hops += [(names[1], 1), (names[1], -1)]
                    elif second == 1 and not odd:
                        hops += [(names[1], 1)]
                    elif second == 3 and odd:
                        hops += [(names[1], -1)]
                    found.append((depth, dx, dy, quarter, hops))
    return found


HOPS = {r[1:4]: r[4] for r in routes()}
N_FORWARD = sum(len(hops) for hops in HOPS.values())
PLACE = [4 * (g // 4) + 2 * (g % 2) + (g // 2) % 2 for g in range(8)]


def onward(piece, hop):
    dx, dy, quarter = piece
    axis, step = hop
    if axis == "x":
        return (dx + step) % RING, dy, quarter
    return dx, (dy + step) % RING, quarter


def further(piece):
    return max([1 + further(onward(piece, hop)) for hop in HOPS[piece]], default=0)


def forwards(piece):
    return sorted(HOPS[piece], key=lambda hop: -further(onward(piece, hop)))


def plan():
    free, arrivals, order = {}, [], []

    def send(piece, hop, now):
        free[hop] = max(free.get(hop, 0.0), now) + 0.7
        heapq.heappush(arrivals, (free[hop] + 1.66, len(order), onward(piece, hop)))

    own = [(0, 0, quarter) for quarter in range(4)]
    first = [(piece, hop) for piece in own for hop in HOPS[piece][:2]]
    first += [(piece, hop) for piece in own for hop in HOPS[piece][2:]]
    for piece, hop in first:
        send(piece, hop, 0.0)
    now = 0.0
    while arrivals:
        when, _, piece = heapq.heappop(arrivals)
        now = max(now, when) + 0.02
        order.append(piece)
        for hop in forwards(piece):
            send(piece, hop, now)
    return order


ORDER = plan()


def semaphores():
    number = {}
    keys = [piece if HOPS[piece] else piece[:2] for piece in ORDER]
    for key in keys:
        number.setdefault(key, len(number))
    return {piece: number[key] for piece, key in zip(ORDER, keys)}, len(number)


SEM, N_SEM = semaphores()
LEAVES = {}
for leaf in ORDER:
    if not HOPS[leaf]:
        LEAVES[leaf[:2]] = LEAVES.get(leaf[:2], 0) + 1
FAR = (2, 1, 3, 0)
PLANE = sorted(
    [(dx, dy) for dx in range(RING) for dy in range(RING)],
    key=lambda o: -min(o[0], RING - o[0]) - min(o[1], RING - o[1]),
)


def kernel(
    hidden,
    keys,
    vals,
    lens,
    ids,
    guid,
    wq,
    kvw,
    wo,
    gain,
    wh,
    out,
    h_c,
    wq_v,
    kvw_v,
    kv_v,
    k_v,
    v_v,
    wo_v,
    wh_v,
    ids_v,
    gain_all,
    part,
    recv_b,
    q_s,
    att_s,
    att_b,
    att_all,
    part_d,
    recv_d,
    resid,
    buf,
    acc,
    ssq,
    counts,
    gcol,
    tot_one,
    tot_all,
    hid_v,
    gain_v,
    lens_v,
    guid_v,
    load_sem,
    w_recv,
    z_recv,
    c_recv,
    f_recv,
    sib_recv,
    one,
):
    S = lax.axis_index("stream")
    D = lax.axis_index("dp")
    T = lax.axis_index("tensor")
    zl, c = T // 2, T % 2
    x, y = D // RING, D % RING
    sib = (S, D, zl * 2 + 1 - c)
    names = ("a", "gain", "b", "c", "d", "t")
    recv_of = {name: one.at[n] for n, name in enumerate(names)}
    departed = one.at[len(names)]

    def remote(src, dst, ssem, rsem, dev):
        copy = pltpu.make_async_remote_copy(
            src_ref=src,
            dst_ref=dst,
            send_sem=ssem,
            recv_sem=rsem,
            device_id=dev,
            device_id_type=MESH,
        )
        copy.start()

    def arrived(ref, rsem):
        pltpu.make_async_remote_copy(
            src_ref=ref,
            dst_ref=ref,
            send_sem=departed,
            recv_sem=rsem,
            device_id=sib,
            device_id_type=MESH,
        ).wait_recv()

    def left(ref):
        pltpu.make_async_remote_copy(
            src_ref=ref,
            dst_ref=ref,
            send_sem=departed,
            recv_sem=recv_of["a"],
            device_id=sib,
            device_id_type=MESH,
        ).wait_send()

    def peer(dx, dy):
        return ((x + dx) % RING) * RING + (y + dy) % RING

    mark("p00_entry")
    barrier = pltpu.get_barrier_semaphore()

    def greet(dev):
        pl.semaphore_signal(barrier, inc=1, device_id=dev, device_id_type=MESH)

    for t in range(TEN):
        greet((1 - S, D, t))
    for dx, dy in PLANE[:-1]:
        greet((S, peer(dx, dy), T))
        greet((S, peer(dx, dy), zl * 2 + 1 - c))
    for i in range(1, TEN):
        greet((S, D, (T + i) % TEN))

    loads = []

    def load(src, dst, sem=None):
        if sem is None:
            sem = load_sem.at[len(loads)]
            loads.append(sem)
        copy = pltpu.make_async_copy(src, dst, sem)
        copy.start()
        return copy

    l_hid = load(hidden.at[0], hid_v)
    load(hidden.at[0, pl.ds(c * 16, 16)], h_c.at[T], recv_of["a"])
    l_gain = load(gain, gain_v)
    l_lens = load(lens, lens_v)
    l_guid = load(guid, guid_v)
    l_wq = load(wq, wq_v.at[c])
    l_kv = load(kvw, kvw_v)
    for g in range(8):
        load(
            ids.at[pl.ds(S * 128 + PLACE[g] * 16, 16), :],
            ids_v.at[pl.ds(g * 16, 16), :],
            load_sem.at[12],
        )
    l_k = load(keys.at[0, :, 0], k_v)
    l_v = load(vals.at[0, :, 0], v_v)
    l_wo = load(wo, wo_v.at[c])
    l_hid.wait()
    pl.semaphore_wait(barrier, 45)

    mark("p01_hidden")
    for dz in (3, 2, 1):
        for core in (0, 1):
            dev = (S, D, ((zl + dz) % 4) * 2 + core)
            remote(
                hid_v.at[pl.ds(core * 16, 16)], h_c.at[T], departed, recv_of["a"], dev
            )
    remote(hid_v.at[pl.ds(16 - c * 16, 16)], h_c.at[T], departed, recv_of["a"], sib)
    remote(wq, wq_v.at[c], departed, w_recv.at[0], sib)
    l_gain.wait()
    gain_all[D] = gain_v[...].astype(F32).reshape(1, 512)
    l_wh = load(wh, wh_v)
    remote(wo, wo_v.at[c], departed, w_recv.at[2], sib)
    l_kv.wait()
    for n in range(2):
        kv_v[c, :, n * 128 : (n + 1) * 128] = kvw_v[:, n, :]
    l_wq.wait()
    remote(kv_v.at[c], kv_v.at[c], departed, w_recv.at[1], sib)
    arrived(h_c, recv_of["a"])

    mark("p02_qkv")
    h = h_c[...].reshape(128, 512)
    for i in range(2):
        g = (c + i) % 2
        if i == 1:
            arrived(wq_v.at[g], w_recv.at[0])
            arrived(kv_v.at[g], w_recv.at[1])
        for n in range(4):
            cols = pl.ds(n * 256, 256)
            r = jnp.dot(h, wq_v[g, :, cols], preferred_element_type=F32)
            part[:, g, :, cols] = r.reshape(8, 16, 256).astype(BF16)
        r = jnp.dot(h, kv_v[g], preferred_element_type=F32)
        part[:, g, :, pl.ds(1024, 256)] = r.reshape(8, 16, 256).astype(BF16)
        for n in range(8):
            to = peer(FAR[n // 2], (y + c) % 2 + 2 - 2 * (n % 2))
            k = to // 2
            if i == 1:
                remote(
                    part.at[k, g], recv_b.at[D], departed, recv_of["b"], (S, to, zl * 2 + g)
                )
                continue

            @pl.when(to == D)
            def _():
                pltpu.make_async_copy(part.at[k, g], recv_b.at[D], recv_of["b"]).start()

            @pl.when(to != D)
            def _():
                remote(
                    part.at[k, g], recv_b.at[D], departed, recv_of["b"], (S, to, zl * 2 + g)
                )
    for i in range(1, DP):
        to = (D + i) % DP
        remote(gain_all.at[D], gain_all.at[D], departed, recv_of["gain"], (S, to, T))

    mark("p03_tables")
    lane = lax.broadcasted_iota(jnp.int32, (16, HEAD), 1)
    row = lax.broadcasted_iota(jnp.int32, (16, HEAD), 0)
    freq = jnp.exp(((lane % 64).astype(F32) * (2.0 / HEAD)) * (-jnp.log(F32(rope_theta))))
    l_lens.wait()
    l_guid.wait()
    position = jnp.zeros((16, HEAD), jnp.int32)
    for p in range(16):
        position = jnp.where(row == p, lens_v[0, p], position)
    angle = position.astype(F32) * freq
    cosine = jnp.cos(angle)
    sine = jnp.sin(angle) * jnp.where(lane < 64, -1.0, 1.0)

    pltpu.make_async_copy(ids.at[pl.ds(0, 128), :], ids_v, load_sem.at[12]).wait()
    base = (D * TEN + T) * 512
    ids_v[...] = jnp.transpose(ids_v[...]) - base
    for n in range(4):
        column = lax.broadcasted_iota(jnp.int32, (128, 128), 0) + n * 128

        def add(r, total):
            for k in range(8):
                here = ids_v[pl.ds(r * 8 + k, 1), :]
                total = total + jnp.where(column == here, 1.0, 0.0)
            return total

        total = lax.fori_loop(0, 16, add, jnp.zeros((128, 128), F32))
        counts[:, pl.ds(n * 128, 128)] = jnp.transpose(total) * penalty_step
    guide = jnp.transpose(jnp.broadcast_to(guid_v[pl.ds(S, 1), :], (128, 128)))
    for g in range(8):
        gcol[g * 16 : (g + 1) * 16] = guide[PLACE[g] * 16 : (PLACE[g] + 1) * 16]

    mark("p04_sumwait")
    arrived(recv_b, recv_of["b"])
    qkv = recv_b[0].astype(F32)
    for i in range(1, DP):
        qkv = qkv + recv_b[i].astype(F32)

    mark("p05_rope")

    def turn(v):
        return v * cosine + pltpu.roll(v, 64, 1) * sine

    for g in range(8):
        q_s[:, g, :] = turn(qkv[:, g * HEAD : (g + 1) * HEAD])
    k_new = turn(qkv[:, 1024:1152]).astype(BF16).astype(F32)
    v_new = qkv[:, 1152:1280].astype(BF16).astype(F32)

    mark("p06_attn")
    l_k.wait()
    l_v.wait()
    scale = HEAD ** (-0.5)
    slot_at = lax.broadcasted_iota(jnp.int32, (8, 256), 1)
    for start in (0, 8):
        prompts = range(start, start + 8)
        q = [q_s[p].astype(BF16) for p in prompts]
        scores = [
            lax.dot_general(
                q[p - start], k_v[p], (((1,), (1,)), ((), ())), preferred_element_type=F32
            )
            for p in prompts
        ]
        k_own = jnp.concatenate([jnp.broadcast_to(k_new[p : p + 1], (8, HEAD)) for p in prompts])
        v_own = jnp.concatenate([jnp.broadcast_to(v_new[p : p + 1], (8, HEAD)) for p in prompts])
        q_all = jnp.concatenate([v.astype(F32) for v in q])
        e_own = jnp.exp(jnp.sum(q_all * k_own, axis=1, keepdims=True) * scale)
        e = jnp.concatenate(
            [
                jnp.where(slot_at < lens_v[0, p], jnp.exp(scores[p - start] * scale), 0.0)
                for p in prompts
            ]
        )
        den = jnp.sum(e, axis=1, keepdims=True) + e_own
        w = (e / den).astype(BF16)
        w_own = (e_own / den).astype(BF16).astype(F32)
        o = jnp.concatenate(
            [
                jnp.dot(
                    w[(p - start) * 8 : (p - start + 1) * 8],
                    v_v[p],
                    preferred_element_type=F32,
                )
                for p in prompts
            ]
        )
        att_s[pl.ds(start, 8)] = (o + w_own * v_own).reshape(8, 8, HEAD)
    for g in range(8):
        att_b[:, pl.ds(g * HEAD, HEAD)] = att_s[:, g, :].astype(BF16)

    mark("p07_gatherC")
    core = D % 2
    slot = c * 8 + D // 2
    for dx, dy in PLANE:
        if (dx, dy) != (0, 0):
            to = peer(dx, dy)
            remote(att_b, att_all.at[slot], departed, c_recv.at[x], (S, to, zl * 2 + core))

    @pl.when(core == c)
    def _():
        pltpu.make_async_copy(att_b, att_all.at[slot], c_recv.at[x]).start()

    @pl.when(core != c)
    def _():
        remote(att_b, att_all.at[slot], departed, c_recv.at[x], sib)

    l_wo.wait()
    arrived(wo_v.at[1 - c], w_recv.at[2])

    for pair in ((2, 1), (3, 0)):
        blocks = [(x + dx) % RING for dx in pair]
        for block in blocks:
            arrived(att_all.at[pl.ds(0, 4)], c_recv.at[block])
        mark(f"p08_outproj{pair[0]}")
        a0 = jnp.concatenate([att_all[pl.ds(2 * b, 2)].reshape(32, 1024) for b in blocks])
        a1 = jnp.concatenate([att_all[pl.ds(8 + 2 * b, 2)].reshape(32, 1024) for b in blocks])
        for n in range(2):
            cols = pl.ds(n * 256, 256)
            r = jnp.dot(a0, wo_v[0, :, cols], preferred_element_type=F32)
            r = r + jnp.dot(a1, wo_v[1, :, cols], preferred_element_type=F32)
            for m, block in enumerate(blocks):
                part_d[block, :, cols] = r[m * 32 : (m + 1) * 32].astype(BF16)
        for block in blocks:
            other = (block // 2 - S) * (block // 2 - S)
            to = (1 - other) * (1 + block % 2) + other * 3 * (block % 2)

            @pl.when(to != zl)
            def _():
                remote(
                    part_d.at[block],
                    recv_d.at[(zl - to + 3) % 4],
                    departed,
                    recv_of["d"],
                    (S, D, to * 2 + c),
                )
        mark(f"p08b_wait{pair[0]}")

    def owned(z):
        inner = ((z + 1) // 2) % 2
        half = inner * S + (1 - inner) * (1 - S)
        return half, 2 * half + inner * (z - 1) + (1 - inner) * (z // 3)

    mark("p09_sumwaitD")
    my_half, mine = owned(zl)
    my_j = 2 * (mine % 2) + c
    total = h_c[pl.ds(2 * mine, 2)].reshape(32, 512).astype(F32) + part_d[mine].astype(F32)
    arrived(recv_d, recv_of["d"])
    for i in range(3):
        total = total + recv_d[i].astype(F32)
    resid[...] = total.astype(BF16)

    mark("p10_z")
    place = buf.at[S, D, pl.ds(my_j * 32, 32), :]
    for turn_z in (2, 1, 3, 0):
        z = (zl + turn_z) % 4
        at_home = jnp.logical_and(my_half == S, 2 * z + S == T)

        @pl.when(at_home)
        def _():
            pltpu.make_async_copy(resid, place, z_recv.at[my_j]).start()

        @pl.when(jnp.logical_not(at_home))
        def _():
            remote(resid, place, departed, z_recv.at[my_j], (my_half, D, 2 * z + S))

    arrived(gain_all.at[pl.ds(0, DP - 1)], recv_of["gain"])
    l_wh.wait()
    acc[...] = jnp.zeros_like(acc)
    ssq[...] = jnp.zeros_like(ssq)

    def neighbour(name, step):
        if name == "x":
            return (S, ((x + RING + step) % RING) * RING + y, T)
        return (S, x * RING + (y + RING + step) % RING, T)

    def slot_of(dx, dy):
        return ((x + RING - dx) % RING) * RING + (y + RING - dy) % RING

    def send_on(piece, hops):
        slot, quarter = slot_of(*piece[:2]), piece[2]
        rows = buf.at[c, slot, pl.ds(quarter * 32, 32), :]
        for hop in hops:
            remote(rows, rows, departed, f_recv.at[SEM[onward(piece, hop)]], neighbour(*hop))

    def share(dx, dy):
        whole = buf.at[c, slot_of(dx, dy)]
        remote(whole, whole, departed, sib_recv.at[slot_of(dx, dy)], sib)

    def head(dx, dy):
        slot = slot_of(dx, dy)
        arrived(buf.at[1 - c, slot], sib_recv.at[slot])
        v = buf[:, slot].reshape(256, 512).astype(F32)
        v2 = v * v
        ssq[...] += v2[:, 0:128] + v2[:, 128:256] + v2[:, 256:384] + v2[:, 384:512]
        w = (v * gain_all[slot]).astype(BF16)
        acc[...] += jnp.dot(
            w,
            wh_v[pl.ds(pl.multiple_of(slot * 512, 512), 512), :],
            preferred_element_type=F32,
        )

    mark("p10b_zwait")
    for quarter in range(4):
        arrived(buf.at[c, D, pl.ds(quarter * 32, 32), :], z_recv.at[quarter])
        send_on((0, 0, quarter), HOPS[(0, 0, quarter)][:2])
    mark("p11_own")
    for quarter in range(4):
        send_on((0, 0, quarter), HOPS[(0, 0, quarter)][2:])
    share(0, 0)
    complete = [(0, (0, 0))]
    held, leaves = {}, {}
    for n, piece in enumerate(ORDER):
        if n % 10 == 0:
            mark(f"p12_pieces{n:02d}")
        dx, dy, quarter = piece
        slot = slot_of(dx, dy)
        if HOPS[piece]:
            arrived(buf.at[c, slot, pl.ds(quarter * 32, 32), :], f_recv.at[SEM[piece]])
            send_on(piece, forwards(piece))
        else:
            leaves[dx, dy] = leaves.get((dx, dy), 0) + 1
            if leaves[dx, dy] == LEAVES[dx, dy]:
                arrived(buf.at[c, slot, pl.ds(0, 32 * LEAVES[dx, dy]), :], f_recv.at[SEM[piece]])
        held[dx, dy] = held.get((dx, dy), 0) + 1
        if held[dx, dy] == 4:
            share(dx, dy)
            complete.append((n, (dx, dy)))
        if complete and n - complete[0][0] >= 8:
            head(*complete.pop(0)[1])
    mark("p13_lastheads")
    for _, offset in complete:
        head(*offset)

    mark("p16_guided")
    inv = lax.rsqrt(jnp.sum(ssq[...], axis=1, keepdims=True) / WIDTH + norm_eps)
    cond = acc[0:128, :] * inv[0:128]
    uncond = acc[128:256, :] * inv[128:256]
    guide = gcol[:, 0:1]
    guided = uncond + guide * (cond - uncond) - counts[...]
    acc[0:128, :] = guided
    e = jnp.exp(guided)
    e = e[:, 0:128] + e[:, 128:256] + e[:, 256:384] + e[:, 384:512]
    mark("p17_total")
    tot_one[...] = jnp.sum(jnp.transpose(e), axis=0, keepdims=True)

    for n, (dx, dy) in enumerate(PLANE):
        for dt in range(TEN):
            if (dx, dy, dt) != (0, 0, 0):
                to = (S, peer(dx, dy), (T + dt) % TEN)
                remote(tot_one, tot_all.at[n * TEN + dt - n // 15], departed, recv_of["t"], to)
    arrived(tot_all, recv_of["t"])
    mark("p18_out")
    totals = tot_one[...] + jnp.sum(tot_all[...], axis=0)
    log_total = jnp.transpose(jnp.broadcast_to(jnp.log(totals), (128, 128)))
    for g in range(8):
        for n in range(4):
            cols = pl.ds(n * 128, 128)
            out[pl.ds(PLACE[g] * 16, 16), cols] = (
                acc[pl.ds(g * 16, 16), cols] - log_total[g * 16 : (g + 1) * 16]
            )

    mark("p19_waitsend")
    left(wq_v.at[0])
    left(kv_v.at[0])
    left(wo_v.at[0])
    left(h_c.at[pl.ds(0, 7)])
    left(gain_all.at[pl.ds(0, DP - 1)])
    left(part_d.at[pl.ds(0, 3)])
    left(buf.at[0, pl.ds(0, 15)])
    left(buf.at[0])
    left(tot_all)
    kept_c = core == c
    kept_z = jnp.logical_and(my_half == S, c == S)

    @pl.when(kept_c)
    def _():
        left(recv_b.at[pl.ds(0, DP - 1)])
        left(att_all.at[pl.ds(0, DP - 1)])

    @pl.when(jnp.logical_not(kept_c))
    def _():
        left(recv_b)
        left(att_all)

    @pl.when(kept_z)
    def _():
        left(part_d.at[pl.ds(0, 3)])

    @pl.when(jnp.logical_not(kept_z))
    def _():
        left(part_d)

    mark(None)


def body(hidden, keys, vals, lens, ids, guid, wq, kvw, wo, gain, wh):
    dma = pltpu.SemaphoreType.DMA
    anywhere = pl.BlockSpec(memory_space=pl.ANY)
    vmem = pl.BlockSpec(memory_space=pltpu.VMEM)
    return pl.pallas_call(
        kernel,
        out_shape=pltpu.VMEM((128, 512), F32),
        in_specs=[anywhere] * 11,
        out_specs=vmem,
        scratch_shapes=[
            pltpu.VMEM((TEN, 16, 512), BF16),
            pltpu.VMEM((2, 512, 1024), BF16),
            pltpu.VMEM((512, 2, 128), BF16),
            pltpu.VMEM((2, 512, 256), BF16),
            pltpu.VMEM((16, 256, 128), BF16),
            pltpu.VMEM((16, 256, 128), BF16),
            pltpu.VMEM((2, 1024, 512), BF16),
            pltpu.VMEM((8192, 512), BF16),
            pltpu.VMEM((128, 128), jnp.int32),
            pltpu.VMEM((DP, 1, 512), F32),
            pltpu.VMEM((8, 2, 16, 1280), BF16),
            pltpu.VMEM((DP, 16, 1280), BF16),
            pltpu.VMEM((16, 8, 128), F32),
            pltpu.VMEM((16, 8, 128), F32),
            pltpu.VMEM((16, 1024), BF16),
            pltpu.VMEM((DP, 16, 1024), BF16),
            pltpu.VMEM((4, 32, 512), BF16),
            pltpu.VMEM((3, 32, 512), BF16),
            pltpu.VMEM((32, 512), BF16),
            pltpu.VMEM((2, DP, 128, 512), BF16),
            pltpu.VMEM((256, 512), F32),
            pltpu.VMEM((256, 128), F32),
            pltpu.VMEM((128, 512), F32),
            pltpu.VMEM((128, 128), F32),
            pltpu.VMEM((1, 128), F32),
            pltpu.VMEM((DP * TEN - 1, 1, 128), F32),
            pltpu.VMEM((32, 512), BF16),
            pltpu.VMEM((512,), BF16),
            pltpu.SMEM((1, 16), jnp.int32),
            pltpu.VMEM((2, 128), F32),
            dma((13,)),
            dma((3,)),
            dma((4,)),
            dma((4,)),
            dma((N_SEM,)),
            dma((DP,)),
            dma((7,)),
        ],
        compiler_params=pltpu.CompilerParams(
            collective_id=0, has_side_effects=True, vmem_limit_bytes=60 * 1024 * 1024
        ),
    )(hidden, keys, vals, lens, ids, guid.reshape(2, 128), wq, kvw, wo, gain, wh)


def solution(mesh):
    return jax.shard_map(
        body,
        mesh=mesh,
        in_specs=(
            P("stream", "tensor", "dp"),
            P("stream", "dp", "tensor", None, None),
            P("stream", "dp", "tensor", None, None),
            P("stream", "dp"),
            P(),
            P(),
            P("dp", "tensor"),
            P("dp", None, "tensor"),
            P("tensor", "dp"),
            P("dp"),
            P(None, ("dp", "tensor")),
        ),
        out_specs=P("stream", ("dp", "tensor")),
        check_vma=False,
    )
```
